512 devices in a mesh: zone: 32 (over x, z_hi, core), period: 16 (over y, z_lo).
Axes of the slice: x: 4, y: 8, z: 8 (z_hi: 4, z_lo: 2; z = z_hi * 2 + z_lo), core: 2. Of those that a mesh axis runs over, the one named last changes fastest.
Arguments:
- x_start: float32 [256, 16, 1600], P('zone', 'period'), may hold values from -6 to 6
- duals: float32 [256, 16, 512], P('zone', 'period'), may hold values from -3 to 3
- cost: float32 [256, 16, 1600], P('zone', 'period'), may hold values from -6 to 6
- hinv: bfloat16 [256, 1600, 1600], P('zone', 'period')
- zone_sizes: int32 [256], P('zone'), may hold values from 640 to 1600, as said below
- partners: int32 [4, 256], P(None, 'zone'), may hold values from 0 to 7, as said below
Outputs:
- primal: float32 [256, 16, 1600], P('zone', 'period')
- dual_out: float32 [256, 16, 512], P('zone', 'period')
The draws below stay inside these ranges and needn't reach their ends.
Inputs may be any that keep to these rules, and one draw needn't show every extreme that they name: `zone_sizes`: each zone has at least its tie and ramp entries live; some zone uses all 1600. In round r the zones of zone index i are paired one to one with the zones of index i XOR 2**(r mod b), b the log2 of the number of zone indices; partners[r, z] is the partner's position among the 8 zones of its index, and the pairing is mutual.
All inputs are finite; a program needn't handle non-finite values.
Results may differ from the reference program's by a relative error of at most 0.0032.
Values may be sent and summed in bfloat16 or wider, within the bound.
No kernel may reach another device: no remote copies, remote signals or barrier semaphores. Data moves between devices by JAX's collectives and lax.ppermute only.
A program may use at most 64 MiB of HBM per device.

```python
import math
import jax
import jax.numpy as jnp
from jax import lax

V = 1600
W = 128
G = 128
ROUNDS = 4
ITERS = 2
Z_DEV = 8
ZONES = 256
PERIODS = 16
N_ZONE = 32


def draw_hinv(key, part):
    first, second = jax.random.split(jax.random.fold_in(key, 11))
    noise = jax.random.normal(first, (ZONES, V, V), jnp.float32)
    symmetric = (noise + jnp.swapaxes(noise, 1, 2)) * (0.2 / math.sqrt(2.0 * V))
    diagonal = jax.random.uniform(second, (ZONES, V, 1), jnp.float32, 0.5, 1.0)
    identity = jnp.arange(V)[:, None] == jnp.arange(V)[None, :]
    return jnp.where(identity[None, :, :], diagonal, symmetric).astype(jnp.bfloat16)


def draw_zone_sizes(key, part):
    first, second = jax.random.split(jax.random.fold_in(key, 23))
    lowest = ROUNDS * W + G
    values = jax.random.randint(first, (ZONES,), lowest, V + 1, dtype=jnp.int32)
    position = jax.random.randint(second, (), 0, ZONES, dtype=jnp.int32)
    values = values.at[position].set(V)
    values = values.at[(position + 1) % ZONES].set(lowest)
    return values.astype(jnp.int32)


def draw_partners(key, part):
    n_devices = ZONES // Z_DEV
    nbits = n_devices.bit_length() - 1
    collected = []
    for round_index in range(ROUNDS):
        keys = jax.random.split(jax.random.fold_in(key, 7 + round_index), n_devices)
        perms = jax.vmap(lambda single: jax.random.permutation(single, Z_DEV))(keys).astype(jnp.int32)
        inverse = jnp.argsort(perms, axis=1).astype(jnp.int32)
        device_ids = jnp.arange(n_devices, dtype=jnp.int32)
        mates = jnp.bitwise_xor(device_ids, jnp.int32(1 << round_index % nbits))
        lower = device_ids < mates
        chosen = jnp.where(lower[:, None], perms, inverse[mates])
        collected.append(chosen.reshape(-1))
    return jnp.stack(collected).astype(jnp.int32)


def block_scale(own_key, shape, cuts, low, largest):
    factor_of, own = 1.0, jax.random.fold_in(own_key, 6)
    for dim, parts in cuts:
        draws = jnp.exp(jax.random.uniform(jax.random.fold_in(own, dim), (parts,), jnp.float32, low / len(cuts), largest / len(cuts)))
        factor_of = factor_of * jnp.repeat(draws, shape[dim] // parts).reshape([-1 if axis == dim else 1 for axis in range(len(shape))])
    return factor_of


def scatter_about(stream_key, shape, deviation, bound, pieces=(), kind=jnp.bfloat16):
    level = block_scale(stream_key, shape, pieces, -0.22, 0.18) if pieces else 1.0
    result = jax.random.normal(stream_key, shape, jnp.float32) * deviation * level
    return jnp.minimum(jnp.maximum(result, -bound), bound).astype(kind)


def setup_inputs(seed: int = 0) -> dict:
    arg_keys = jax.random.split(jax.random.key(seed), 7)
    return {
        "x_start": scatter_about(arg_keys[0], (ZONES, PERIODS, V), 1.0, 6.0, ((0, 32), (1, 16)), jnp.float32),
        "duals": scatter_about(arg_keys[1], (ZONES, PERIODS, ROUNDS * W), 0.5, 3.0, ((0, 32), (1, 16)), jnp.float32),
        "cost": scatter_about(arg_keys[2], (ZONES, PERIODS, V), 1.0, 6.0, ((0, 32), (1, 16)), jnp.float32),
        "hinv": draw_hinv(jax.random.fold_in(arg_keys[6], 71), 0),
        "zone_sizes": draw_zone_sizes(jax.random.fold_in(arg_keys[6], 71), 0),
        "partners": draw_partners(jax.random.fold_in(arg_keys[6], 71), 0),
    }


rho_ties = 1.0
prox_weight = 0.5
ramp_weight = 0.5


def apply_inverse(pair):
    matrix, right = pair
    return jnp.dot(right, matrix.T, preferred_element_type=jnp.float32)


def reference(x_start, duals, cost, hinv, zone_sizes, partners):
    nbits = N_ZONE.bit_length() - 1
    zone_ids = jnp.arange(ZONES, dtype=jnp.int32)
    device_of = zone_ids // Z_DEV
    live_mask = (jnp.arange(V, dtype=jnp.int32)[None, :] < zone_sizes[:, None]).astype(jnp.float32)[:, None, :]
    current = x_start
    dual_state = duals
    tie_end = ROUNDS * W
    for iteration in range(ITERS):
        tie_terms = []
        new_duals = []
        for round_index in range(ROUNDS):
            mates = jnp.bitwise_xor(device_of, jnp.int32(1 << (round_index % nbits))) * Z_DEV + partners[round_index]
            own_block = current[:, :, round_index * W:(round_index + 1) * W]
            partner_block = jnp.take(own_block, mates.astype(jnp.int32), axis=0)
            old_dual = dual_state[:, :, round_index * W:(round_index + 1) * W]
            updated = old_dual + rho_ties * 0.5 * (own_block - partner_block)
            new_duals.append(updated)
            tie_terms.append(rho_ties * 0.5 * (own_block + partner_block) - updated)
        dual_state = jnp.concatenate(new_duals, axis=2)
        ramp_block = current[:, :, tie_end:tie_end + G]
        padded = jnp.pad(ramp_block, ((0, 0), (1, 1), (0, 0)))
        ramp_term = ramp_weight * (padded[:, :-2] + padded[:, 2:])
        filler = jnp.zeros((ZONES, PERIODS, V - tie_end - G), jnp.float32)
        addition = jnp.concatenate(tie_terms + [ramp_term, filler], axis=2)
        right_side = ((prox_weight * current - cost + addition) * live_mask).astype(jnp.bfloat16)
        product = lax.map(apply_inverse, (hinv, right_side))
        current = product * live_mask
    return current, dual_state
```

```python
import functools
import itertools

import jax
import jax.numpy as jnp
from jax import lax
from jax.experimental import pallas as pl
from jax.experimental.pallas import tpu as pltpu
from jax.sharding import Mesh, PartitionSpec as P

V = 1600
W = 128
ROUNDS = 4
TIE = ROUNDS * W
RAMP = TIE + W
Z = 8
T = 16
ROWS = V // T
VP = 1664
BW = VP + 3 * W
DW = VP + 2 * W
AXES = ("xh", "xl", "zh", "core", "y", "zl")
SIZES = (2, 2, 4, 2, 8, 2)
ZONE = ("xh", "xl", "zh", "core")
NEAR = ("xl", "zh", "core")
PERIOD = ("y", "zl")
FIRST = {0: 0, 1: 1, 2: 2, 3: 2, 4: 3, 5: 3}
SECOND = {1: 0, 2: 1, 3: 3}


def near_index():
    return (lax.axis_index("xl") * 4 + lax.axis_index("zh")) * 2 + lax.axis_index("core")


def period_index():
    return lax.axis_index("y") * 2 + lax.axis_index("zl")


def swap_route(rounds):
    route = []
    for place in itertools.product(*[range(size) for size in SIZES]):
        xh, xl, zh, core, y, zl = place
        k = y * 2 + zl
        if k in rounds:
            zone = ((xh * 2 + xl) * 4 + zh) * 2 + core
            mate = zone ^ (1 << rounds[k])
            there = (mate >> 4, (mate >> 3) & 1, (mate >> 1) & 3, mate & 1, y, zl)
            ends = []
            for spot in (place, there):
                flat = 0
                for size, index in zip(SIZES, spot):
                    flat = flat * size + index
                ends.append(flat)
            route.append(tuple(ends))
    return route


def rounded(values):
    return values.astype(jnp.bfloat16)


def two_parts(values):
    high = rounded(values)
    return high, rounded(values - high.astype(jnp.float32))


def tie_blocks_kernel(x_ref, out_ref):
    me = near_index()
    out_ref[...] = jnp.zeros_like(out_ref)
    x = x_ref[:, 0, :TIE]
    for r in range(ROUNDS):
        slot = pl.multiple_of((me ^ (1 << r)) * Z, Z)
        out_ref[pl.ds(slot, Z), :] = x[:, r * W : (r + 1) * W]


def first_side_kernel(sizes_ref, partners_ref, x_ref, dual_ref, cost_ref, ties_ref, out_ref, dual_out_ref):
    me = near_index()
    x = x_ref[:, 0, :]
    cost = cost_ref[:, 0, :]
    dual = dual_ref[:, 0, :]
    lane = lax.broadcasted_iota(jnp.int32, (1, V), 1)
    live = jnp.concatenate([(lane < sizes_ref[z]).astype(jnp.float32) for z in range(Z)], axis=0)
    terms, new_duals = [], []
    for r in range(ROUNDS):
        own = x[:, r * W : (r + 1) * W]
        slot = (me ^ (1 << r)) * Z
        other = jnp.concatenate([ties_ref[pl.ds(slot + partners_ref[r, z], 1), :] for z in range(Z)], axis=0)
        updated = dual[:, r * W : (r + 1) * W] + 0.5 * (own - other)
        new_duals.append(updated)
        terms.append(0.5 * (own + other) - updated)
    new_dual = jnp.concatenate(new_duals, axis=1)
    rest = jnp.zeros((Z, V - TIE), jnp.float32)
    right = (0.5 * x - cost + jnp.concatenate(terms + [rest], axis=1)) * live
    dual_out_ref[...] = new_dual
    later = cost + jnp.concatenate([new_dual, rest], axis=1)
    later_high, later_low = two_parts(later)
    common = jnp.concatenate(
        [rounded(right), jnp.zeros((Z, VP - V), jnp.bfloat16), rounded(x[:, TIE:RAMP])], axis=1
    )
    blank = jnp.zeros((Z, W - ROWS), jnp.bfloat16)
    for k in range(T):
        own_rows = slice(k * ROWS, (k + 1) * ROWS)
        out_ref[k * Z : (k + 1) * Z, :] = jnp.concatenate(
            [common, later_high[:, own_rows], blank, later_low[:, own_rows], blank], axis=1
        )


def next_period(values):
    edge = jnp.zeros((Z, values.shape[1]), values.dtype)
    return jnp.concatenate([values[Z:], edge], axis=0)


def last_period(values):
    edge = jnp.zeros((Z, values.shape[1]), values.dtype)
    return jnp.concatenate([edge, values[:-Z]], axis=0)


def first_product_kernel(sizes_ref, block_ref, hinv_ref, out_ref):
    first = period_index() * ROWS
    ramp = block_ref[:, VP : VP + W].astype(jnp.float32)
    ramp_side = block_ref[:, TIE:RAMP].astype(jnp.float32) + 0.5 * (last_period(ramp) + next_period(ramp))
    side = jnp.concatenate([block_ref[:, :TIE], rounded(ramp_side), block_ref[:, RAMP:V]], axis=1)
    row = lax.broadcasted_iota(jnp.int32, (T * Z, ROWS), 0) & (Z - 1)
    lane = lax.broadcasted_iota(jnp.int32, (T * Z, ROWS), 1) + first
    total = jnp.zeros((T * Z, ROWS), jnp.float32)
    for z in range(Z):
        product = lax.dot_general(
            side, hinv_ref[z], (((1,), (1,)), ((), ())), preferred_element_type=jnp.float32
        )
        total = jnp.where((row == z) & (lane < sizes_ref[z]), product, total)
    out_ref[...] = jnp.concatenate([total, jnp.zeros((T * Z, W - ROWS), jnp.float32)], axis=1)


def second_product_kernel(sizes_ref, partners_ref, block_ref, current_ref, one_ref, two_ref, hinv_ref, out_ref):
    k = period_index()
    first = k * ROWS
    first_round = jnp.where(k == 0, 0, jnp.where(k == 1, 1, jnp.where(k <= 3, 2, 3)))
    second_round = jnp.where(k == 1, 0, jnp.where(k == 2, 1, jnp.where(k == 3, 3, 0)))
    current = current_ref[...]
    later = block_ref[:, VP + W : VP + 2 * W].astype(jnp.float32) + block_ref[:, VP + 2 * W :].astype(jnp.float32)
    zone = lax.broadcasted_iota(jnp.int32, (Z, W), 0)
    column = lax.broadcasted_iota(jnp.int32, (Z, W), 1)

    def from_partner(received_ref, round_index):
        partner = jnp.zeros((Z, W), jnp.int32)
        for z in range(Z):
            partner = jnp.where(zone == z, partners_ref[round_index, z], partner)
        pick = jnp.concatenate(
            [(column - p * Z == partner).astype(jnp.float32) for p in range(T)], axis=0
        )
        return jnp.dot(
            pick, received_ref[...], preferred_element_type=jnp.float32, precision=lax.Precision.HIGHEST
        )

    row = lax.broadcasted_iota(jnp.int32, (T * Z, W), 0) & (Z - 1)
    lane = lax.broadcasted_iota(jnp.int32, (T * Z, W), 1)
    entry = lane + first
    round_of = entry >> 7
    tie = entry < TIE
    other = jnp.where(
        round_of == first_round,
        from_partner(one_ref, first_round),
        from_partner(two_ref, second_round),
    )
    ramp = 0.5 * (last_period(current) + next_period(current))
    addition = jnp.where(tie, other, jnp.where(entry < RAMP, ramp, 0.0))
    right = 0.5 * current - later + addition
    size = jnp.zeros((T * Z, W), jnp.int32)
    for z in range(Z):
        size = jnp.where(row == z, sizes_ref[z], size)
    right = rounded(jnp.where((entry < size) & (lane < ROWS), right, 0.0))[:, :ROWS]
    step_high, step_low = two_parts(jnp.where(tie, 0.5 * (current - other), 0.0))
    out_ref[:, VP : VP + W] = step_high
    out_ref[:, VP + W :] = step_low
    row = row[:, :ROWS]
    total = jnp.zeros((T * Z, V), jnp.float32)
    for z in range(Z):
        total = total + jnp.dot(
            jnp.where(row == z, right, jnp.zeros_like(right)), hinv_ref[z], preferred_element_type=jnp.float32
        )
    out_ref[:, :V] = rounded(total)
    out_ref[:, V:VP] = jnp.zeros((T * Z, VP - V), jnp.bfloat16)


def last_sum_kernel(sizes_ref, block_ref, dual_ref, primal_ref, dual_out_ref):
    lane = lax.broadcasted_iota(jnp.int32, (1, V), 1)
    live = jnp.concatenate([(lane < sizes_ref[z]).astype(jnp.float32) for z in range(Z)], axis=0)
    total = jnp.zeros((Z, V), jnp.float32)
    for k in range(T):
        total = total + block_ref[k * Z : (k + 1) * Z, :V].astype(jnp.float32)
    primal_ref[:, 0, :] = total * live
    steps = []
    for k in range(-(-TIE // ROWS)):
        part = block_ref[k * Z : (k + 1) * Z, VP : VP + W].astype(jnp.float32) + block_ref[
            k * Z : (k + 1) * Z, VP + W :
        ].astype(jnp.float32)
        steps.append(part[:, : min(ROWS, TIE - k * ROWS)])
    dual_out_ref[:, 0, :] = dual_ref[...] + jnp.concatenate(steps, axis=1)


SMEM = pl.BlockSpec(memory_space=pltpu.SMEM)
VMEM = pl.BlockSpec(memory_space=pltpu.VMEM)


def call(kernel, name, in_specs, out_shape):
    many = isinstance(out_shape, tuple)
    return pl.pallas_call(
        kernel,
        name=name,
        in_specs=in_specs,
        out_specs=tuple(VMEM for _ in out_shape) if many else VMEM,
        out_shape=out_shape,
    )


def shards(x, duals, cost, hinv, sizes, partners):
    shape = jax.ShapeDtypeStruct
    f32, bf16 = jnp.float32, jnp.bfloat16
    ties = call(tie_blocks_kernel, "tie_blocks", [VMEM], shape((T * Z, W), f32))(x)
    ties = lax.all_to_all(ties, NEAR, 0, 0, tiled=True)
    block, dual = call(
        first_side_kernel,
        "first_side",
        [SMEM, SMEM, VMEM, VMEM, VMEM, VMEM],
        (shape((T * Z, BW), bf16), shape((Z, TIE), f32)),
    )(sizes, partners, x, duals, cost, ties)
    block = lax.all_to_all(block, PERIOD, 0, 0, tiled=True)
    current = call(first_product_kernel, "first_product", [SMEM, VMEM, VMEM], shape((T * Z, W), f32))(
        sizes, block, hinv
    )
    one = lax.ppermute(current, AXES, swap_route(FIRST))
    two = lax.ppermute(current, AXES, swap_route(SECOND))
    block = call(
        second_product_kernel,
        "second_product",
        [SMEM, SMEM, VMEM, VMEM, VMEM, VMEM, VMEM],
        shape((T * Z, DW), bf16),
    )(sizes, partners, block, current, one, two, hinv)
    block = lax.all_to_all(block, PERIOD, 0, 0, tiled=True)
    return call(
        last_sum_kernel, "last_sum", [SMEM, VMEM, VMEM], (shape((Z, 1, V), f32), shape((Z, 1, TIE), f32))
    )(sizes, block, dual)


def solution(mesh):
    fine = Mesh(mesh.devices.reshape(SIZES), AXES)
    whole = P(ZONE, PERIOD, None)
    return jax.shard_map(
        shards,
        mesh=fine,
        in_specs=(whole, whole, whole, whole, P(ZONE), P(None, ZONE)),
        out_specs=(whole, whole),
        check_vma=False,
    )
```

```python
import functools
import itertools

import jax
import jax.numpy as jnp
from jax import lax
from jax.experimental import pallas as pl
from jax.experimental.pallas import tpu as pltpu
from jax.sharding import Mesh, PartitionSpec as P

V = 1600
W = 128
ROUNDS = 4
TIE = ROUNDS * W
RAMP = TIE + W
Z = 8
T = 16
ROWS = V // T
VP = 1664
BW = VP + 3 * W
DW = VP + 2 * W
AXES = ("xh", "xl", "zh", "core", "y", "zl")
SIZES = (2, 2, 4, 2, 8, 2)
ZONE = ("xh", "xl", "zh", "core")
NEAR = ("xl", "zh", "core")
PERIOD = ("y", "zl")
FIRST = {0: 0, 1: 1, 2: 2, 3: 2, 4: 3, 5: 3}
SECOND = {1: 0, 2: 1, 3: 3}


def near_index():
    return (lax.axis_index("xl") * 4 + lax.axis_index("zh")) * 2 + lax.axis_index("core")


def period_index():
    return lax.axis_index("y") * 2 + lax.axis_index("zl")


def swap_route(rounds):
    route = []
    for place in itertools.product(*[range(size) for size in SIZES]):
        xh, xl, zh, core, y, zl = place
        k = y * 2 + zl
        if k in rounds:
            zone = ((xh * 2 + xl) * 4 + zh) * 2 + core
            mate = zone ^ (1 << rounds[k])
            there = (mate >> 4, (mate >> 3) & 1, (mate >> 1) & 3, mate & 1, y, zl)
            ends = []
            for spot in (place, there):
                flat = 0
                for size, index in zip(SIZES, spot):
                    flat = flat * size + index
                ends.append(flat)
            route.append(tuple(ends))
    return route


def rounded(values):
    return values.astype(jnp.bfloat16)


def two_parts(values):
    high = rounded(values)
    return high, rounded(values - high.astype(jnp.float32))


def tie_blocks_kernel(x_ref, out_ref):
    me = near_index()
    out_ref[...] = jnp.zeros_like(out_ref)
    x = x_ref[:, 0, :TIE]
    for r in range(ROUNDS):
        slot = pl.multiple_of((me ^ (1 << r)) * Z, Z)
        out_ref[pl.ds(slot, Z), :] = x[:, r * W : (r + 1) * W]


def first_side_kernel(sizes_ref, partners_ref, x_ref, dual_ref, cost_ref, ties_ref, out_ref, dual_out_ref):
    me = near_index()
    x = x_ref[:, 0, :]
    cost = cost_ref[:, 0, :]
    dual = dual_ref[:, 0, :]
    lane = lax.broadcasted_iota(jnp.int32, (1, V), 1)
    live = jnp.concatenate([(lane < sizes_ref[z]).astype(jnp.float32) for z in range(Z)], axis=0)
    terms, new_duals = [], []
    for r in range(ROUNDS):
        own = x[:, r * W : (r + 1) * W]
        slot = (me ^ (1 << r)) * Z
        other = jnp.concatenate([ties_ref[pl.ds(slot + partners_ref[r, z], 1), :] for z in range(Z)], axis=0)
        updated = dual[:, r * W : (r + 1) * W] + 0.5 * (own - other)
        new_duals.append(updated)
        terms.append(0.5 * (own + other) - updated)
    new_dual = jnp.concatenate(new_duals, axis=1)
    rest = jnp.zeros((Z, V - TIE), jnp.float32)
    right = (0.5 * x - cost + jnp.concatenate(terms + [rest], axis=1)) * live
    dual_out_ref[...] = new_dual
    later = cost + jnp.concatenate([new_dual, rest], axis=1)
    later_high, later_low = two_parts(later)
    common = jnp.concatenate(
        [rounded(right), jnp.zeros((Z, VP - V), jnp.bfloat16), rounded(x[:, TIE:RAMP])], axis=1
    )
    blank = jnp.zeros((Z, W - ROWS), jnp.bfloat16)
    for k in range(T):
        own_rows = slice(k * ROWS, (k + 1) * ROWS)
        out_ref[k * Z : (k + 1) * Z, :] = jnp.concatenate(
            [common, later_high[:, own_rows], blank, later_low[:, own_rows], blank], axis=1
        )


def next_period(values):
    edge = jnp.zeros((Z, values.shape[1]), values.dtype)
    return jnp.concatenate([values[Z:], edge], axis=0)


def last_period(values):
    edge = jnp.zeros((Z, values.shape[1]), values.dtype)
    return jnp.concatenate([edge, values[:-Z]], axis=0)


def first_product_kernel(sizes_ref, block_ref, hinv_ref, out_ref):
    first = period_index() * ROWS
    ramp = block_ref[:, VP : VP + W].astype(jnp.float32)
    ramp_side = block_ref[:, TIE:RAMP].astype(jnp.float32) + 0.5 * (last_period(ramp) + next_period(ramp))
    side = jnp.concatenate([block_ref[:, :TIE], rounded(ramp_side), block_ref[:, RAMP:V]], axis=1)
    row = lax.broadcasted_iota(jnp.int32, (T * Z, ROWS), 0) & (Z - 1)
    lane = lax.broadcasted_iota(jnp.int32, (T * Z, ROWS), 1) + first
    total = jnp.zeros((T * Z, ROWS), jnp.float32)
    for z in range(Z):
        product = lax.dot_general(
            side, hinv_ref[z], (((1,), (1,)), ((), ())), preferred_element_type=jnp.float32
        )
        total = jnp.where((row == z) & (lane < sizes_ref[z]), product, total)
    out_ref[...] = jnp.concatenate([total, jnp.zeros((T * Z, W - ROWS), jnp.float32)], axis=1)


def second_product_kernel(sizes_ref, partners_ref, block_ref, current_ref, one_ref, two_ref, hinv_ref, out_ref):
    k = period_index()
    first = k * ROWS
    first_round = jnp.where(k == 0, 0, jnp.where(k == 1, 1, jnp.where(k <= 3, 2, 3)))
    second_round = jnp.where(k == 1, 0, jnp.where(k == 2, 1, jnp.where(k == 3, 3, 0)))
    current = current_ref[...]
    later = block_ref[:, VP + W : VP + 2 * W].astype(jnp.float32) + block_ref[:, VP + 2 * W :].astype(jnp.float32)
    zone = lax.broadcasted_iota(jnp.int32, (Z, W), 0)
    column = lax.broadcasted_iota(jnp.int32, (Z, W), 1)

    def from_partner(received_ref, round_index):
        partner = jnp.zeros((Z, W), jnp.int32)
        for z in range(Z):
            partner = jnp.where(zone == z, partners_ref[round_index, z], partner)
        pick = jnp.concatenate(
            [(column - p * Z == partner).astype(jnp.float32) for p in range(T)], axis=0
        )
        return jnp.dot(
            pick, received_ref[...], preferred_element_type=jnp.float32, precision=lax.Precision.HIGHEST
        )

    row = lax.broadcasted_iota(jnp.int32, (T * Z, W), 0) & (Z - 1)
    lane = lax.broadcasted_iota(jnp.int32, (T * Z, W), 1)
    entry = lane + first
    round_of = entry >> 7
    tie = entry < TIE
    other = jnp.where(
        round_of == first_round,
        from_partner(one_ref, first_round),
        from_partner(two_ref, second_round),
    )
    ramp = 0.5 * (last_period(current) + next_period(current))
    addition = jnp.where(tie, other, jnp.where(entry < RAMP, ramp, 0.0))
    right = 0.5 * current - later + addition
    size = jnp.zeros((T * Z, W), jnp.int32)
    for z in range(Z):
        size = jnp.where(row == z, sizes_ref[z], size)
    right = rounded(jnp.where((entry < size) & (lane < ROWS), right, 0.0))[:, :ROWS]
    step_high, step_low = two_parts(jnp.where(tie, 0.5 * (current - other), 0.0))
    out_ref[:, VP : VP + W] = step_high
    out_ref[:, VP + W :] = step_low
    row = row[:, :ROWS]
    total = jnp.zeros((T * Z, V), jnp.float32)
    for z in range(Z):
        total = total + jnp.dot(
            jnp.where(row == z, right, jnp.zeros_like(right)), hinv_ref[z], preferred_element_type=jnp.float32
        )
    out_ref[:, :V] = rounded(total)
    out_ref[:, V:VP] = jnp.zeros((T * Z, VP - V), jnp.bfloat16)


def last_sum_kernel(sizes_ref, block_ref, dual_ref, primal_ref, dual_out_ref):
    lane = lax.broadcasted_iota(jnp.int32, (1, V), 1)
    live = jnp.concatenate([(lane < sizes_ref[z]).astype(jnp.float32) for z in range(Z)], axis=0)
    total = jnp.zeros((Z, V), jnp.float32)
    for k in range(T):
        total = total + block_ref[k * Z : (k + 1) * Z, :V].astype(jnp.float32)
    primal_ref[:, 0, :] = total * live
    steps = []
    for k in range(-(-TIE // ROWS)):
        part = block_ref[k * Z : (k + 1) * Z, VP : VP + W].astype(jnp.float32) + block_ref[
            k * Z : (k + 1) * Z, VP + W :
        ].astype(jnp.float32)
        steps.append(part[:, : min(ROWS, TIE - k * ROWS)])
    dual_out_ref[:, 0, :] = dual_ref[...] + jnp.concatenate(steps, axis=1)


SMEM = pl.BlockSpec(memory_space=pltpu.SMEM)
VMEM = pl.BlockSpec(memory_space=pltpu.VMEM)


def call(kernel, name, in_specs, out_shape):
    many = isinstance(out_shape, tuple)
    return pl.pallas_call(
        kernel,
        name=name,
        in_specs=in_specs,
        out_specs=tuple(VMEM for _ in out_shape) if many else VMEM,
        out_shape=out_shape,
        compiler_params=pltpu.CompilerParams(vmem_limit_bytes=16 << 20),
    )


def near(values):
    return pltpu.with_memory_space_constraint(values, pltpu.VMEM)


def shards(x, duals, cost, hinv, sizes, partners):
    f32, bf16 = jnp.float32, jnp.bfloat16
    x, duals, cost, hinv = near(x), near(duals), near(cost), near(hinv)
    ties = call(tie_blocks_kernel, "tie_blocks", [VMEM], pltpu.VMEM((T * Z, W), f32))(x)
    ties = near(lax.all_to_all(ties, NEAR, 0, 0, tiled=True))
    block, dual = call(
        first_side_kernel,
        "first_side",
        [SMEM, SMEM, VMEM, VMEM, VMEM, VMEM],
        (pltpu.VMEM((T * Z, BW), bf16), pltpu.VMEM((Z, TIE), f32)),
    )(sizes, partners, x, duals, cost, ties)
    block = near(lax.all_to_all(block, PERIOD, 0, 0, tiled=True))
    current = call(first_product_kernel, "first_product", [SMEM, VMEM, VMEM], pltpu.VMEM((T * Z, W), f32))(
        sizes, block, hinv
    )
    one = near(lax.ppermute(current, AXES, swap_route(FIRST)))
    two = near(lax.ppermute(current, AXES, swap_route(SECOND)))
    block = call(
        second_product_kernel,
        "second_product",
        [SMEM, SMEM, VMEM, VMEM, VMEM, VMEM, VMEM],
        pltpu.VMEM((T * Z, DW), bf16),
    )(sizes, partners, block, current, one, two, hinv)
    block = near(lax.all_to_all(block, PERIOD, 0, 0, tiled=True))
    shape = jax.ShapeDtypeStruct
    return call(
        last_sum_kernel, "last_sum", [SMEM, VMEM, VMEM], (shape((Z, 1, V), f32), shape((Z, 1, TIE), f32))
    )(sizes, block, dual)


def solution(mesh):
    fine = Mesh(mesh.devices.reshape(SIZES), AXES)
    whole = P(ZONE, PERIOD, None)
    return jax.shard_map(
        shards,
        mesh=fine,
        in_specs=(whole, whole, whole, whole, P(ZONE), P(None, ZONE)),
        out_specs=(whole, whole),
        check_vma=False,
    )
```

```python
import itertools

import jax
import jax.numpy as jnp
from jax import lax
from jax.experimental import pallas as pl
from jax.experimental.pallas import tpu as pltpu
from jax.sharding import Mesh, PartitionSpec as P

V = 1600
W = 128
ROUNDS = 4
TIE = ROUNDS * W
RAMP = TIE + W
Z = 8
T = 16
ROWS = V // T
VP = 1664
BW = VP + 3 * W
RP = 104
SIZE_ROW, SIZE_LANE, MATE_ROW = 0, Z, 2 * Z
MATE_LANE = MATE_ROW + ROUNDS * Z
META = MATE_LANE + ROUNDS * Z
DW = VP + 2 * W
AXES = ("xh", "xl", "zh", "core", "y", "zl")
SIZES = (2, 2, 4, 2, 8, 2)
ZONE = ("xh", "xl", "zh", "core")
NEAR = ("xl", "zh", "core")
PERIOD = ("y", "zl")
FIRST = {0: 0, 1: 1, 2: 2, 3: 2, 4: 3, 5: 3}
SECOND = {1: 0, 2: 1, 3: 3}


def near_index():
    return (lax.axis_index("xl") * 4 + lax.axis_index("zh")) * 2 + lax.axis_index("core")


def period_index():
    return lax.axis_index("y") * 2 + lax.axis_index("zl")


def swap_route(rounds):
    route = []
    for place in itertools.product(*[range(size) for size in SIZES]):
        xh, xl, zh, core, y, zl = place
        k = y * 2 + zl
        if k in rounds:
            zone = ((xh * 2 + xl) * 4 + zh) * 2 + core
            mate = zone ^ (1 << rounds[k])
            there = (mate >> 4, (mate >> 3) & 1, (mate >> 1) & 3, mate & 1, y, zl)
            ends = []
            for spot in (place, there):
                flat = 0
                for size, index in zip(SIZES, spot):
                    flat = flat * size + index
                ends.append(flat)
            route.append(tuple(ends))
    return route


def rounded(values):
    return values.astype(jnp.bfloat16)


def two_parts(values):
    high = rounded(values)
    return high, rounded(values - high.astype(jnp.float32))


def fetch_kernel(x_hbm, dual_hbm, cost_hbm, sizes_hbm, partners_hbm, ties_ref, x_ref, dual_ref, cost_ref, meta_ref, sizes_ref, partners_ref, sems):
    pairs = ((x_hbm, x_ref), (sizes_hbm, sizes_ref), (partners_hbm, partners_ref), (dual_hbm, dual_ref), (cost_hbm, cost_ref))
    copies = [pltpu.make_async_copy(here, there, sems.at[i]) for i, (here, there) in enumerate(pairs)]
    for copy in copies:
        copy.start()
    me = near_index()
    ties_ref[...] = jnp.zeros_like(ties_ref)
    row = lax.broadcasted_iota(jnp.int32, (Z, W), 0)
    lane = lax.broadcasted_iota(jnp.int32, (Z, W), 1) & (Z - 1)
    for copy in copies[:3]:
        copy.wait()
    x = x_ref[:, 0, :TIE]
    for r in range(ROUNDS):
        slot = pl.multiple_of((me ^ (1 << r)) * Z, Z)
        ties_ref[pl.ds(slot, Z), :] = x[:, r * W : (r + 1) * W]

    def spread(index, value):
        out = jnp.zeros((Z, W), jnp.int32)
        for z in range(Z):
            out = jnp.where(index == z, value(z), out)
        return out

    meta_ref[SIZE_ROW : SIZE_ROW + Z, :] = spread(row, lambda z: sizes_ref[z])
    meta_ref[SIZE_LANE : SIZE_LANE + Z, :] = spread(lane, lambda z: sizes_ref[z])
    for r in range(ROUNDS):
        at = MATE_ROW + r * Z
        meta_ref[at : at + Z, :] = spread(row, lambda z: partners_ref[r, z])
        at = MATE_LANE + r * Z
        meta_ref[at : at + Z, :] = spread(lane, lambda z: partners_ref[r, z])
    for copy in copies[3:]:
        copy.wait()


def live_rows(meta_ref):
    lane = lax.broadcasted_iota(jnp.int32, (Z, VP), 1)
    size = jnp.concatenate([meta_ref[SIZE_ROW : SIZE_ROW + Z, :]] * (VP // W), axis=1)
    return (lane < size).astype(jnp.float32)[:, :V]


def first_side_kernel(meta_ref, x_ref, dual_ref, cost_ref, ties_ref, hinv_hbm, out_ref, dual_out_ref, hinv_ref, sem):
    fetch = pltpu.make_async_copy(hinv_hbm, hinv_ref, sem)
    fetch.start()
    me = near_index()
    x = x_ref[:, 0, :]
    cost = cost_ref[:, 0, :]
    dual = dual_ref[:, 0, :]
    terms, new_duals = [], []
    for r in range(ROUNDS):
        own = x[:, r * W : (r + 1) * W]
        slot = (me ^ (1 << r)) * Z
        mate = meta_ref[MATE_ROW + r * Z : MATE_ROW + (r + 1) * Z, :]
        other = jnp.zeros((Z, W), jnp.float32)
        for z in range(Z):
            other = jnp.where(mate == z, ties_ref[pl.ds(slot + z, 1), :], other)
        updated = dual[:, r * W : (r + 1) * W] + 0.5 * (own - other)
        new_duals.append(updated)
        terms.append(0.5 * (own + other) - updated)
    new_dual = jnp.concatenate(new_duals, axis=1)
    rest = jnp.zeros((Z, V - TIE), jnp.float32)
    right = (0.5 * x - cost + jnp.concatenate(terms + [rest], axis=1)) * live_rows(meta_ref)
    dual_out_ref[...] = new_dual
    later = cost + jnp.concatenate([new_dual, rest], axis=1)
    later_high, later_low = two_parts(later)
    common = jnp.concatenate(
        [rounded(right), jnp.zeros((Z, VP - V), jnp.bfloat16), rounded(x[:, TIE:RAMP])], axis=1
    )
    blank = jnp.zeros((Z, W - ROWS), jnp.bfloat16)
    for k in range(T):
        own_rows = slice(k * ROWS, (k + 1) * ROWS)
        out_ref[k * Z : (k + 1) * Z, :] = jnp.concatenate(
            [common, later_high[:, own_rows], blank, later_low[:, own_rows], blank], axis=1
        )
    fetch.wait()


def zone_match():
    row = lax.broadcasted_iota(jnp.int32, (Z, T * Z), 0)
    lane = lax.broadcasted_iota(jnp.int32, (Z, T * Z), 1)
    return row == (lane & (Z - 1))


def first_product_kernel(meta_ref, block_ref, hinv_ref, out_ref):
    first = period_index() * ROWS
    ramp = block_ref[:, VP : VP + W].astype(jnp.float32)
    edge = jnp.zeros((Z, W), jnp.float32)
    around = jnp.concatenate([edge, ramp[:-Z]], axis=0) + jnp.concatenate([ramp[Z:], edge], axis=0)
    ramp_side = block_ref[:, TIE:RAMP].astype(jnp.float32) + 0.5 * around
    side = jnp.concatenate([block_ref[:, :TIE], rounded(ramp_side), block_ref[:, RAMP:V]], axis=1)
    product = lax.dot_general(
        hinv_ref[...], side, (((1,), (1,)), ((), ())), preferred_element_type=jnp.float32
    ).reshape(ROWS, Z, T * Z)
    current = jnp.sum(jnp.where(zone_match()[None], product, 0.0), axis=1)
    row = lax.broadcasted_iota(jnp.int32, (ROWS, T * Z), 0) + first
    size = meta_ref[SIZE_LANE : SIZE_LANE + 1, :]
    out_ref[:ROWS, :] = jnp.where(row < size, current, 0.0)
    out_ref[ROWS:, :] = jnp.zeros((RP - ROWS, T * Z), jnp.float32)


def second_product_kernel(meta_ref, block_ref, current_ref, one_ref, two_ref, hinv_ref, out_ref):
    k = period_index()
    first_round = jnp.where(k == 0, 0, jnp.where(k == 1, 1, jnp.where(k <= 3, 2, 3)))
    second_round = jnp.where(k == 1, 0, jnp.where(k == 2, 1, jnp.where(k == 3, 3, 0)))
    current = current_ref[...]
    later = block_ref[:, VP + W : VP + 2 * W].astype(jnp.float32) + block_ref[:, VP + 2 * W :].astype(jnp.float32)
    later = later.T[:RP]
    place = lax.broadcasted_iota(jnp.int32, (T * Z, T * Z), 0)
    group = lax.broadcasted_iota(jnp.int32, (T * Z, T * Z), 1) & ~(Z - 1)

    def pick(round_index):
        mate = meta_ref[pl.ds(MATE_LANE + round_index * Z, 1), :]
        return (place == group + mate).astype(jnp.float32)

    row = lax.broadcasted_iota(jnp.int32, (RP, T * Z), 0)
    lane = lax.broadcasted_iota(jnp.int32, (RP, T * Z), 1)
    entry = row + k * ROWS
    round_of = entry >> 7
    tie = entry < TIE
    received = jnp.concatenate(
        [
            jnp.where(tie & (round_of == first_round), one_ref[...], 0.0),
            jnp.where(tie & (round_of == second_round) & (k >= 1) & (k <= 3), two_ref[...], 0.0),
        ],
        axis=1,
    )
    picks = jnp.concatenate([pick(first_round), pick(second_round)], axis=0)
    other = jnp.dot(received, picks, preferred_element_type=jnp.float32, precision=lax.Precision.HIGHEST)
    before = jnp.where(lane < Z, 0.0, pltpu.roll(current, Z, 1))
    after = jnp.where(lane >= (T - 1) * Z, 0.0, pltpu.roll(current, (T - 1) * Z, 1))
    ramp = jnp.where((entry >= TIE) & (entry < RAMP), 0.5 * (before + after), 0.0)
    right = 0.5 * current - later + jnp.where(tie, other, ramp)
    size = meta_ref[SIZE_LANE : SIZE_LANE + 1, :]
    right = jnp.where(entry < size, right, 0.0)[:ROWS]
    side = rounded(jnp.where(zone_match()[None], right[:, None, :], 0.0).reshape(ROWS * Z, T * Z))
    step = jnp.where(tie, 0.5 * (current - other), 0.0)
    step = jnp.concatenate([step, jnp.zeros((W - RP, T * Z), jnp.float32)], axis=0).T
    step_high, step_low = two_parts(step)
    out_ref[:, VP : VP + W] = step_high
    out_ref[:, VP + W :] = step_low
    total = lax.dot_general(side, hinv_ref[...], (((0,), (0,)), ((), ())), preferred_element_type=jnp.float32)
    out_ref[:, :V] = rounded(total)
    out_ref[:, V:VP] = jnp.zeros((T * Z, VP - V), jnp.bfloat16)


def last_sum_kernel(meta_ref, block_ref, dual_ref, primal_ref, dual_out_ref):
    total = jnp.zeros((Z, V), jnp.float32)
    for k in range(T):
        total = total + block_ref[k * Z : (k + 1) * Z, :V].astype(jnp.float32)
    primal_ref[:, 0, :] = total * live_rows(meta_ref)
    steps = []
    for k in range(-(-TIE // ROWS)):
        part = block_ref[k * Z : (k + 1) * Z, VP : VP + W].astype(jnp.float32) + block_ref[
            k * Z : (k + 1) * Z, VP + W :
        ].astype(jnp.float32)
        steps.append(part[:, : min(ROWS, TIE - k * ROWS)])
    dual_out_ref[:, 0, :] = dual_ref[...] + jnp.concatenate(steps, axis=1)


HBM = pl.BlockSpec(memory_space=pltpu.HBM)
VMEM = pl.BlockSpec(memory_space=pltpu.VMEM)


def call(kernel, name, in_specs, out_shape, scratch=()):
    many = isinstance(out_shape, tuple)
    return pl.pallas_call(
        kernel,
        name=name,
        in_specs=in_specs,
        out_specs=tuple(VMEM for _ in out_shape) if many else VMEM,
        out_shape=out_shape,
        scratch_shapes=scratch,
        compiler_params=pltpu.CompilerParams(vmem_limit_bytes=16 << 20),
    )


def near(values):
    return pltpu.with_memory_space_constraint(values, pltpu.VMEM)


def far(values):
    return pltpu.with_memory_space_constraint(values, pltpu.HBM)


def shards(x, duals, cost, hinv, sizes, partners):
    f32, bf16 = jnp.float32, jnp.bfloat16
    hinv = jnp.transpose(hinv, (1, 0, 2)).reshape(ROWS * Z, V)
    ties, x, duals, cost, meta = call(
        fetch_kernel,
        "fetch",
        [HBM] * 5,
        (
            pltpu.VMEM((T * Z, W), f32),
            pltpu.VMEM((Z, 1, V), f32),
            pltpu.VMEM((Z, 1, TIE), f32),
            pltpu.VMEM((Z, 1, V), f32),
            pltpu.VMEM((META, W), jnp.int32),
        ),
        [pltpu.SMEM((Z,), jnp.int32), pltpu.SMEM((ROUNDS, Z), jnp.int32), pltpu.SemaphoreType.DMA((5,))],
    )(far(x), far(duals), far(cost), far(sizes), far(partners))
    ties = near(lax.all_to_all(ties, NEAR, 0, 0, tiled=True))
    block, dual, hinv = call(
        first_side_kernel,
        "first_side",
        [VMEM] * 5 + [HBM],
        (pltpu.VMEM((T * Z, BW), bf16), pltpu.VMEM((Z, TIE), f32), pltpu.VMEM((ROWS * Z, V), bf16)),
        [pltpu.SemaphoreType.DMA],
    )(meta, x, duals, cost, ties, far(hinv))
    block = near(lax.all_to_all(block, PERIOD, 0, 0, tiled=True))
    current = call(first_product_kernel, "first_product", [VMEM] * 3, pltpu.VMEM((RP, T * Z), f32))(
        meta, block, hinv
    )
    one = near(lax.ppermute(current, AXES, swap_route(FIRST)))
    two = near(lax.ppermute(current, AXES, swap_route(SECOND)))
    block = call(second_product_kernel, "second_product", [VMEM] * 6, pltpu.VMEM((T * Z, DW), bf16))(
        meta, block, current, one, two, hinv
    )
    block = near(lax.all_to_all(block, PERIOD, 0, 0, tiled=True))
    shape = jax.ShapeDtypeStruct
    return call(last_sum_kernel, "last_sum", [VMEM] * 3, (shape((Z, 1, V), f32), shape((Z, 1, TIE), f32)))(
        meta, block, dual
    )


def solution(mesh):
    fine = Mesh(mesh.devices.reshape(SIZES), AXES)
    whole = P(ZONE, PERIOD, None)
    return jax.shard_map(
        shards,
        mesh=fine,
        in_specs=(whole, whole, whole, whole, P(ZONE), P(None, ZONE)),
        out_specs=(whole, whole),
        check_vma=False,
    )
```

```python
import itertools

import jax
import jax.numpy as jnp
from jax import lax
from jax.experimental import pallas as pl
from jax.experimental.pallas import tpu as pltpu
from jax.sharding import Mesh, PartitionSpec as P

V = 1600
W = 128
ROUNDS = 4
TIE = ROUNDS * W
RAMP = TIE + W
Z = 8
T = 16
ROWS = V // T
VP = 1664
LOW = 92
TAIL = 1536
RAMP_AT = V + ROWS + LOW
BW = RAMP_AT + W
RP = 104
SIZE_ROW, SIZE_LANE, MATE_ROW = 0, Z, 2 * Z
MATE_LANE = MATE_ROW + ROUNDS * Z
META = MATE_LANE + ROUNDS * Z
DW = VP + W
AXES = ("xh", "xl", "zh", "core", "y", "zl")
SIZES = (2, 2, 4, 2, 8, 2)
ZONE = ("xh", "xl", "zh", "core")
NEAR = ("xl", "zh", "core")
PERIOD = ("y", "zl")
FIRST = {0: 0, 1: 1, 2: 2, 3: 2, 4: 3, 5: 3}
SECOND = {1: 0, 2: 1, 3: 3}


def near_index():
    return (lax.axis_index("xl") * 4 + lax.axis_index("zh")) * 2 + lax.axis_index("core")


def period_index():
    return lax.axis_index("y") * 2 + lax.axis_index("zl")


def swap_route(rounds):
    route = []
    for place in itertools.product(*[range(size) for size in SIZES]):
        xh, xl, zh, core, y, zl = place
        k = y * 2 + zl
        if k in rounds:
            zone = ((xh * 2 + xl) * 4 + zh) * 2 + core
            mate = zone ^ (1 << rounds[k])
            there = (mate >> 4, (mate >> 3) & 1, (mate >> 1) & 3, mate & 1, y, zl)
            ends = []
            for spot in (place, there):
                flat = 0
                for size, index in zip(SIZES, spot):
                    flat = flat * size + index
                ends.append(flat)
            route.append(tuple(ends))
    return route


def rounded(values):
    return values.astype(jnp.bfloat16)


def fetch_kernel(x_hbm, dual_hbm, cost_hbm, sizes_hbm, partners_hbm, ties_ref, x_ref, dual_ref, cost_ref, meta_ref, sizes_ref, partners_ref, sems):
    pairs = ((x_hbm, x_ref), (sizes_hbm, sizes_ref), (partners_hbm, partners_ref), (dual_hbm, dual_ref), (cost_hbm, cost_ref))
    copies = [pltpu.make_async_copy(here, there, sems.at[i]) for i, (here, there) in enumerate(pairs)]
    for copy in copies:
        copy.start()
    me = near_index()
    ties_ref[...] = jnp.zeros_like(ties_ref)
    row = lax.broadcasted_iota(jnp.int32, (Z, W), 0)
    lane = lax.broadcasted_iota(jnp.int32, (Z, W), 1) & (Z - 1)
    for copy in copies[:3]:
        copy.wait()
    x = x_ref[:, 0, :TIE]
    for r in range(ROUNDS):
        slot = pl.multiple_of((me ^ (1 << r)) * Z, Z)
        ties_ref[pl.ds(slot, Z), :] = x[:, r * W : (r + 1) * W]

    def spread(index, value):
        out = jnp.zeros((Z, W), jnp.int32)
        for z in range(Z):
            out = jnp.where(index == z, value(z), out)
        return out

    meta_ref[SIZE_ROW : SIZE_ROW + Z, :] = spread(row, lambda z: sizes_ref[z])
    meta_ref[SIZE_LANE : SIZE_LANE + Z, :] = spread(lane, lambda z: sizes_ref[z])
    for r in range(ROUNDS):
        at = MATE_ROW + r * Z
        meta_ref[at : at + Z, :] = spread(row, lambda z: partners_ref[r, z])
        at = MATE_LANE + r * Z
        meta_ref[at : at + Z, :] = spread(lane, lambda z: partners_ref[r, z])
    for copy in copies[3:]:
        copy.wait()


def live_rows(meta_ref):
    lane = lax.broadcasted_iota(jnp.int32, (Z, VP), 1)
    size = jnp.concatenate([meta_ref[SIZE_ROW : SIZE_ROW + Z, :]] * (VP // W), axis=1)
    return (lane < size).astype(jnp.float32)[:, :V]


def first_side_kernel(meta_ref, x_ref, dual_ref, cost_ref, ties_ref, hinv_hbm, out_ref, dual_out_ref, hinv_ref, sem):
    fetch = pltpu.make_async_copy(hinv_hbm, hinv_ref, sem)
    fetch.start()
    me = near_index()
    x = x_ref[:, 0, :]
    cost = cost_ref[:, 0, :]
    dual = dual_ref[:, 0, :]
    terms, new_duals = [], []
    for r in range(ROUNDS):
        own = x[:, r * W : (r + 1) * W]
        slot = (me ^ (1 << r)) * Z
        mate = meta_ref[MATE_ROW + r * Z : MATE_ROW + (r + 1) * Z, :]
        other = jnp.zeros((Z, W), jnp.float32)
        for z in range(Z):
            other = jnp.where(mate == z, ties_ref[pl.ds(slot + z, 1), :], other)
        updated = dual[:, r * W : (r + 1) * W] + 0.5 * (own - other)
        new_duals.append(updated)
        terms.append(0.5 * (own + other) - updated)
    new_dual = jnp.concatenate(new_duals, axis=1)
    rest = jnp.zeros((Z, V - TIE), jnp.float32)
    right = (0.5 * x - cost + jnp.concatenate(terms + [rest], axis=1)) * live_rows(meta_ref)
    dual_out_ref[...] = new_dual
    later = cost + jnp.concatenate([new_dual, rest], axis=1)
    later_high = rounded(later).astype(jnp.float32)
    later_low = later - later_high
    head, ramp = rounded(right[:, :TAIL]), rounded(x[:, TIE:RAMP])
    for k in range(T):
        at = k * ROWS
        tail = [right[:, TAIL:], later_high[:, at : at + ROWS], later_low[:, at : at + LOW]]
        out_ref[k * Z : (k + 1) * Z, :] = jnp.concatenate(
            [head, rounded(jnp.concatenate(tail, axis=1)), ramp], axis=1
        )
    fetch.wait()


def zone_match():
    row = lax.broadcasted_iota(jnp.int32, (Z, T * Z), 0)
    lane = lax.broadcasted_iota(jnp.int32, (Z, T * Z), 1)
    return row == (lane & (Z - 1))


def first_product_kernel(meta_ref, block_ref, hinv_ref, out_ref):
    first = period_index() * ROWS
    ramp = block_ref[:, RAMP_AT:].astype(jnp.float32)
    edge = jnp.zeros((Z, W), jnp.float32)
    around = jnp.concatenate([edge, ramp[:-Z]], axis=0) + jnp.concatenate([ramp[Z:], edge], axis=0)
    ramp_side = block_ref[:, TIE:RAMP].astype(jnp.float32) + 0.5 * around
    side = jnp.concatenate([block_ref[:, :TIE], rounded(ramp_side), block_ref[:, RAMP:V]], axis=1)
    product = lax.dot_general(
        hinv_ref[...], side, (((1,), (1,)), ((), ())), preferred_element_type=jnp.float32
    ).reshape(ROWS, Z, T * Z)
    current = jnp.sum(jnp.where(zone_match()[None], product, 0.0), axis=1)
    row = lax.broadcasted_iota(jnp.int32, (ROWS, T * Z), 0) + first
    size = meta_ref[SIZE_LANE : SIZE_LANE + 1, :]
    out_ref[:ROWS, :] = jnp.where(row < size, current, 0.0)
    out_ref[ROWS:, :] = jnp.zeros((RP - ROWS, T * Z), jnp.float32)


def second_product_kernel(meta_ref, block_ref, current_ref, two_ref, one_ref, hinv_ref, out_ref):
    k = period_index()
    first_round = jnp.where(k == 0, 0, jnp.where(k == 1, 1, jnp.where(k <= 3, 2, 3)))
    second_round = jnp.where(k == 1, 0, jnp.where(k == 2, 1, jnp.where(k == 3, 3, 0)))
    current = current_ref[...]
    later = block_ref[:, TAIL:RAMP_AT].astype(jnp.float32).T[V - TAIL :]
    blank = jnp.zeros((RP - LOW, T * Z), jnp.float32)
    later = jnp.concatenate([later[:ROWS], blank[: RP - ROWS]], axis=0) + jnp.concatenate([later[ROWS:], blank], axis=0)
    place = lax.broadcasted_iota(jnp.int32, (T * Z, T * Z), 0)
    group = lax.broadcasted_iota(jnp.int32, (T * Z, T * Z), 1) & ~(Z - 1)

    def pick(round_index):
        mate = meta_ref[pl.ds(MATE_LANE + round_index * Z, 1), :]
        return (place == group + mate).astype(jnp.float32)

    row = lax.broadcasted_iota(jnp.int32, (RP, T * Z), 0)
    lane = lax.broadcasted_iota(jnp.int32, (RP, T * Z), 1)
    entry = row + k * ROWS
    round_of = entry >> 7
    tie = entry < TIE
    received = jnp.concatenate(
        [
            jnp.where(tie & (round_of == first_round), one_ref[...], 0.0),
            jnp.where(tie & (round_of == second_round) & (k >= 1) & (k <= 3), two_ref[...], 0.0),
        ],
        axis=1,
    )
    picks = jnp.concatenate([pick(first_round), pick(second_round)], axis=0)
    other = jnp.dot(received, picks, preferred_element_type=jnp.float32, precision=lax.Precision.HIGHEST)
    before = jnp.where(lane < Z, 0.0, pltpu.roll(current, Z, 1))
    after = jnp.where(lane >= (T - 1) * Z, 0.0, pltpu.roll(current, (T - 1) * Z, 1))
    ramp = jnp.where((entry >= TIE) & (entry < RAMP), 0.5 * (before + after), 0.0)
    right = 0.5 * current - later + jnp.where(tie, other, ramp)
    size = meta_ref[SIZE_LANE : SIZE_LANE + 1, :]
    right = jnp.where(entry < size, right, 0.0)[:ROWS]
    side = rounded(jnp.where(zone_match()[None], right[:, None, :], 0.0).reshape(ROWS * Z, T * Z))
    step = jnp.where(tie, 0.5 * (current - other), 0.0)
    step = jnp.concatenate([step, jnp.zeros((W - RP, T * Z), jnp.float32)], axis=0).T
    out_ref[:, VP:] = rounded(step)
    total = lax.dot_general(side, hinv_ref[...], (((0,), (0,)), ((), ())), preferred_element_type=jnp.float32)
    out_ref[:, :V] = rounded(total)
    out_ref[:, V:VP] = jnp.zeros((T * Z, VP - V), jnp.bfloat16)


def last_sum_kernel(meta_ref, block_ref, dual_ref, primal_ref, dual_out_ref):
    total = jnp.zeros((Z, V), jnp.float32)
    for k in range(T):
        total = total + block_ref[k * Z : (k + 1) * Z, :V].astype(jnp.float32)
    primal_ref[:, 0, :] = total * live_rows(meta_ref)
    steps = []
    for k in range(-(-TIE // ROWS)):
        part = block_ref[k * Z : (k + 1) * Z, VP:].astype(jnp.float32)
        steps.append(part[:, : min(ROWS, TIE - k * ROWS)])
    dual_out_ref[:, 0, :] = dual_ref[...] + jnp.concatenate(steps, axis=1)


HBM = pl.BlockSpec(memory_space=pltpu.HBM)
VMEM = pl.BlockSpec(memory_space=pltpu.VMEM)


def call(kernel, name, in_specs, out_shape, scratch=()):
    many = isinstance(out_shape, tuple)
    return pl.pallas_call(
        kernel,
        name=name,
        in_specs=in_specs,
        out_specs=tuple(VMEM for _ in out_shape) if many else VMEM,
        out_shape=out_shape,
        scratch_shapes=scratch,
        compiler_params=pltpu.CompilerParams(vmem_limit_bytes=16 << 20),
    )


def near(values):
    return pltpu.with_memory_space_constraint(values, pltpu.VMEM)


def far(values):
    return pltpu.with_memory_space_constraint(values, pltpu.HBM)


def shards(x, duals, cost, hinv, sizes, partners):
    f32, bf16 = jnp.float32, jnp.bfloat16
    hinv = jnp.transpose(hinv, (1, 0, 2)).reshape(ROWS * Z, V)
    ties, x, duals, cost, meta = call(
        fetch_kernel,
        "fetch",
        [HBM] * 5,
        (
            pltpu.VMEM((T * Z, W), f32),
            pltpu.VMEM((Z, 1, V), f32),
            pltpu.VMEM((Z, 1, TIE), f32),
            pltpu.VMEM((Z, 1, V), f32),
            pltpu.VMEM((META, W), jnp.int32),
        ),
        [pltpu.SMEM((Z,), jnp.int32), pltpu.SMEM((ROUNDS, Z), jnp.int32), pltpu.SemaphoreType.DMA((5,))],
    )(far(x), far(duals), far(cost), far(sizes), far(partners))
    ties = near(lax.all_to_all(ties, NEAR, 0, 0, tiled=True))
    block, dual, hinv = call(
        first_side_kernel,
        "first_side",
        [VMEM] * 5 + [HBM],
        (pltpu.VMEM((T * Z, BW), bf16), pltpu.VMEM((Z, TIE), f32), pltpu.VMEM((ROWS * Z, V), bf16)),
        [pltpu.SemaphoreType.DMA],
    )(meta, x, duals, cost, ties, far(hinv))
    block = near(lax.all_to_all(block, PERIOD, 0, 0, tiled=True))
    current = call(first_product_kernel, "first_product", [VMEM] * 3, pltpu.VMEM((RP, T * Z), f32))(
        meta, block, hinv
    )
    two = near(lax.ppermute(current, AXES, swap_route(SECOND)))
    one = near(lax.ppermute(current, AXES, swap_route(FIRST)))
    block = call(second_product_kernel, "second_product", [VMEM] * 6, pltpu.VMEM((T * Z, DW), bf16))(
        meta, block, current, two, one, hinv
    )
    block = near(lax.all_to_all(block, PERIOD, 0, 0, tiled=True))
    shape = jax.ShapeDtypeStruct
    return call(last_sum_kernel, "last_sum", [VMEM] * 3, (shape((Z, 1, V), f32), shape((Z, 1, TIE), f32)))(
        meta, block, dual
    )


def solution(mesh):
    fine = Mesh(mesh.devices.reshape(SIZES), AXES)
    whole = P(ZONE, PERIOD, None)
    return jax.shard_map(
        shards,
        mesh=fine,
        in_specs=(whole, whole, whole, whole, P(ZONE), P(None, ZONE)),
        out_specs=(whole, whole),
        check_vma=False,
    )
```

```python
import itertools

import jax
import jax.numpy as jnp
from jax import lax
from jax.experimental import pallas as pl
from jax.experimental.pallas import tpu as pltpu
from jax.sharding import Mesh, PartitionSpec as P

V = 1600
W = 128
ROUNDS = 4
TIE = ROUNDS * W
RAMP = TIE + W
Z = 8
T = 16
ROWS = V // T
VP = 1664
LOW = 92
TAIL = 1536
RAMP_AT = V + ROWS + LOW
BW = RAMP_AT + W
RP = 104
SIZE_ROW, SIZE_LANE, MATE_ROW = 0, Z, 2 * Z
MATE_LANE = MATE_ROW + ROUNDS * Z
META = MATE_LANE + ROUNDS * Z
DW = VP + W
AXES = ("xh", "xl", "zh", "core", "y", "zl")
SIZES = (2, 2, 4, 2, 8, 2)
ZONE = ("xh", "xl", "zh", "core")
NEAR = ("xl", "zh", "core")
PERIOD = ("y", "zl")
SLOTS = ("zl", "y")
ORDER = tuple(range(0, T, 2)) + tuple(range(1, T, 2))
HALF = T * Z // 2
SECOND_ROWS = 56
FIRST = {0: 0, 1: 1, 2: 2, 3: 2, 4: 3, 5: 3}
SECOND = {1: 0, 2: 1, 3: 3}


def near_index():
    return (lax.axis_index("xl") * 4 + lax.axis_index("zh")) * 2 + lax.axis_index("core")


def period_index():
    return lax.axis_index("y") * 2 + lax.axis_index("zl")


def swap_route(rounds):
    route = []
    for place in itertools.product(*[range(size) for size in SIZES]):
        xh, xl, zh, core, y, zl = place
        k = y * 2 + zl
        if k in rounds:
            zone = ((xh * 2 + xl) * 4 + zh) * 2 + core
            mate = zone ^ (1 << rounds[k])
            there = (mate >> 4, (mate >> 3) & 1, (mate >> 1) & 3, mate & 1, y, zl)
            ends = []
            for spot in (place, there):
                flat = 0
                for size, index in zip(SIZES, spot):
                    flat = flat * size + index
                ends.append(flat)
            route.append(tuple(ends))
    return route


def rounded(values):
    return values.astype(jnp.bfloat16)


def fetch_kernel(x_hbm, dual_hbm, cost_hbm, sizes_hbm, partners_hbm, ties_ref, x_ref, dual_ref, cost_ref, meta_ref, sizes_ref, partners_ref, sems):
    pairs = ((x_hbm, x_ref), (sizes_hbm, sizes_ref), (partners_hbm, partners_ref), (dual_hbm, dual_ref), (cost_hbm, cost_ref))
    copies = [pltpu.make_async_copy(here, there, sems.at[i]) for i, (here, there) in enumerate(pairs)]
    for copy in copies:
        copy.start()
    me = near_index()
    ties_ref[...] = jnp.zeros_like(ties_ref)
    row = lax.broadcasted_iota(jnp.int32, (Z, W), 0)
    lane = lax.broadcasted_iota(jnp.int32, (Z, W), 1) & (Z - 1)
    for copy in copies[:3]:
        copy.wait()
    x = x_ref[:, 0, :TIE]
    for r in range(ROUNDS):
        slot = pl.multiple_of((me ^ (1 << r)) * Z, Z)
        ties_ref[pl.ds(slot, Z), :] = x[:, r * W : (r + 1) * W]

    def spread(index, value):
        out = jnp.zeros((Z, W), jnp.int32)
        for z in range(Z):
            out = jnp.where(index == z, value(z), out)
        return out

    meta_ref[SIZE_ROW : SIZE_ROW + Z, :] = spread(row, lambda z: sizes_ref[z])
    meta_ref[SIZE_LANE : SIZE_LANE + Z, :] = spread(lane, lambda z: sizes_ref[z])
    for r in range(ROUNDS):
        at = MATE_ROW + r * Z
        meta_ref[at : at + Z, :] = spread(row, lambda z: partners_ref[r, z])
        at = MATE_LANE + r * Z
        meta_ref[at : at + Z, :] = spread(lane, lambda z: partners_ref[r, z])
    for copy in copies[3:]:
        copy.wait()


def live_rows(meta_ref):
    lane = lax.broadcasted_iota(jnp.int32, (Z, VP), 1)
    size = jnp.concatenate([meta_ref[SIZE_ROW : SIZE_ROW + Z, :]] * (VP // W), axis=1)
    return (lane < size).astype(jnp.float32)[:, :V]


def first_side_kernel(meta_ref, x_ref, dual_ref, cost_ref, ties_ref, hinv_hbm, out_ref, dual_out_ref, hinv_ref, sem):
    fetch = pltpu.make_async_copy(hinv_hbm, hinv_ref, sem)
    fetch.start()
    me = near_index()
    x = x_ref[:, 0, :]
    cost = cost_ref[:, 0, :]
    dual = dual_ref[:, 0, :]
    terms, new_duals = [], []
    for r in range(ROUNDS):
        own = x[:, r * W : (r + 1) * W]
        slot = (me ^ (1 << r)) * Z
        mate = meta_ref[MATE_ROW + r * Z : MATE_ROW + (r + 1) * Z, :]
        other = jnp.zeros((Z, W), jnp.float32)
        for z in range(Z):
            other = jnp.where(mate == z, ties_ref[pl.ds(slot + z, 1), :], other)
        updated = dual[:, r * W : (r + 1) * W] + 0.5 * (own - other)
        new_duals.append(updated)
        terms.append(0.5 * (own + other) - updated)
    new_dual = jnp.concatenate(new_duals, axis=1)
    rest = jnp.zeros((Z, V - TIE), jnp.float32)
    right = (0.5 * x - cost + jnp.concatenate(terms + [rest], axis=1)) * live_rows(meta_ref)
    dual_out_ref[...] = new_dual
    later = cost + jnp.concatenate([new_dual, rest], axis=1)
    later_high = rounded(later).astype(jnp.float32)
    later_low = later - later_high
    head, ramp = rounded(right[:, :TAIL]), rounded(x[:, TIE:RAMP])
    for slot, k in enumerate(ORDER):
        at = k * ROWS
        tail = [right[:, TAIL:], later_high[:, at : at + ROWS], later_low[:, at : at + LOW]]
        out_ref[slot * Z : (slot + 1) * Z, :] = jnp.concatenate(
            [head, rounded(jnp.concatenate(tail, axis=1)), ramp], axis=1
        )
    fetch.wait()


def zone_match():
    row = lax.broadcasted_iota(jnp.int32, (Z, T * Z), 0)
    lane = lax.broadcasted_iota(jnp.int32, (Z, T * Z), 1)
    return row == (lane & (Z - 1))


def first_product_kernel(meta_ref, block_ref, hinv_ref, out_ref, second_ref):
    first = period_index() * ROWS
    ramp = block_ref[:, RAMP_AT:].astype(jnp.float32)
    edge = jnp.zeros((Z, W), jnp.float32)
    even, odd = ramp[:HALF], ramp[HALF:]
    around = jnp.concatenate(
        [
            odd + jnp.concatenate([edge, odd[:-Z]], axis=0),
            even + jnp.concatenate([even[Z:], edge], axis=0),
        ],
        axis=0,
    )
    ramp_side = block_ref[:, TIE:RAMP].astype(jnp.float32) + 0.5 * around
    side = jnp.concatenate([block_ref[:, :TIE], rounded(ramp_side), block_ref[:, RAMP:V]], axis=1)
    product = lax.dot_general(
        hinv_ref[...], side, (((1,), (1,)), ((), ())), preferred_element_type=jnp.float32
    ).reshape(ROWS, Z, T * Z)
    current = jnp.sum(jnp.where(zone_match()[None], product, 0.0), axis=1)
    row = lax.broadcasted_iota(jnp.int32, (ROWS, T * Z), 0) + first
    size = meta_ref[SIZE_LANE : SIZE_LANE + 1, :]
    current = jnp.where(row < size, current, 0.0)
    current = jnp.concatenate([current, jnp.zeros((RP - ROWS, T * Z), jnp.float32)], axis=0)
    out_ref[...] = current
    second_ref[...] = jnp.where(period_index() == 3, current[RP - SECOND_ROWS :], current[:SECOND_ROWS])


def second_product_kernel(meta_ref, block_ref, current_ref, two_ref, one_ref, hinv_ref, out_ref):
    k = period_index()
    first_round = jnp.where(k == 0, 0, jnp.where(k == 1, 1, jnp.where(k <= 3, 2, 3)))
    second_round = jnp.where(k == 1, 0, jnp.where(k == 2, 1, jnp.where(k == 3, 3, 0)))
    current = current_ref[...]
    later = block_ref[:, TAIL:RAMP_AT].astype(jnp.float32).T[V - TAIL :]
    blank = jnp.zeros((RP - LOW, T * Z), jnp.float32)
    later = jnp.concatenate([later[:ROWS], blank[: RP - ROWS]], axis=0) + jnp.concatenate([later[ROWS:], blank], axis=0)
    place = lax.broadcasted_iota(jnp.int32, (T * Z, T * Z), 0)
    group = lax.broadcasted_iota(jnp.int32, (T * Z, T * Z), 1) & ~(Z - 1)

    def pick(round_index):
        mate = meta_ref[pl.ds(MATE_LANE + round_index * Z, 1), :]
        return (place == group + mate).astype(jnp.float32)

    row = lax.broadcasted_iota(jnp.int32, (RP, T * Z), 0)
    lane = lax.broadcasted_iota(jnp.int32, (RP, T * Z), 1)
    entry = row + k * ROWS
    round_of = entry >> 7
    tie = entry < TIE
    blank = jnp.zeros((RP - SECOND_ROWS, T * Z), jnp.float32)
    second = jnp.where(
        k == 3,
        jnp.concatenate([blank, two_ref[...]], axis=0),
        jnp.concatenate([two_ref[...], blank], axis=0),
    )
    received = jnp.concatenate(
        [
            jnp.where(tie & (round_of == first_round), one_ref[...], 0.0),
            jnp.where(tie & (round_of == second_round) & (k >= 1) & (k <= 3), second, 0.0),
        ],
        axis=1,
    )
    picks = jnp.concatenate([pick(first_round), pick(second_round)], axis=0)
    other = jnp.dot(received, picks, preferred_element_type=jnp.float32, precision=lax.Precision.HIGHEST)
    beside = pltpu.roll(current, HALF, 1)
    before = jnp.where(lane < Z, 0.0, pltpu.roll(beside, Z, 1))
    after = jnp.where(lane >= (T - 1) * Z, 0.0, pltpu.roll(beside, (T - 1) * Z, 1))
    ramp = jnp.where((entry >= TIE) & (entry < RAMP), 0.5 * (beside + jnp.where(lane < HALF, before, after)), 0.0)
    right = 0.5 * current - later + jnp.where(tie, other, ramp)
    size = meta_ref[SIZE_LANE : SIZE_LANE + 1, :]
    right = jnp.where(entry < size, right, 0.0)[:ROWS]
    side = rounded(jnp.where(zone_match()[None], right[:, None, :], 0.0).reshape(ROWS * Z, T * Z))
    step = jnp.where(tie, 0.5 * (current - other), 0.0)
    step = jnp.concatenate([step, jnp.zeros((W - RP, T * Z), jnp.float32)], axis=0).T
    out_ref[:, VP:] = rounded(step)
    total = lax.dot_general(side, hinv_ref[...], (((0,), (0,)), ((), ())), preferred_element_type=jnp.float32)
    out_ref[:, :V] = rounded(total)
    out_ref[:, V:VP] = jnp.zeros((T * Z, VP - V), jnp.bfloat16)


def last_sum_kernel(meta_ref, block_ref, dual_ref, primal_ref, dual_out_ref):
    total = jnp.zeros((Z, V), jnp.float32)
    for k in range(T):
        total = total + block_ref[k * Z : (k + 1) * Z, :V].astype(jnp.float32)
    primal_ref[:, 0, :] = total * live_rows(meta_ref)
    steps = []
    for k in range(-(-TIE // ROWS)):
        slot = ORDER.index(k)
        part = block_ref[slot * Z : (slot + 1) * Z, VP:].astype(jnp.float32)
        steps.append(part[:, : min(ROWS, TIE - k * ROWS)])
    dual_out_ref[:, 0, :] = dual_ref[...] + jnp.concatenate(steps, axis=1)


HBM = pl.BlockSpec(memory_space=pltpu.HBM)
VMEM = pl.BlockSpec(memory_space=pltpu.VMEM)


def call(kernel, name, in_specs, out_shape, scratch=()):
    many = isinstance(out_shape, tuple)
    return pl.pallas_call(
        kernel,
        name=name,
        in_specs=in_specs,
        out_specs=tuple(VMEM for _ in out_shape) if many else VMEM,
        out_shape=out_shape,
        scratch_shapes=scratch,
        compiler_params=pltpu.CompilerParams(vmem_limit_bytes=16 << 20),
    )


def near(values):
    return pltpu.with_memory_space_constraint(values, pltpu.VMEM)


def far(values):
    return pltpu.with_memory_space_constraint(values, pltpu.HBM)


def shards(x, duals, cost, hinv, sizes, partners):
    f32, bf16 = jnp.float32, jnp.bfloat16
    hinv = jnp.transpose(hinv, (1, 0, 2)).reshape(ROWS * Z, V)
    ties, x, duals, cost, meta = call(
        fetch_kernel,
        "fetch",
        [HBM] * 5,
        (
            pltpu.VMEM((T * Z, W), f32),
            pltpu.VMEM((Z, 1, V), f32),
            pltpu.VMEM((Z, 1, TIE), f32),
            pltpu.VMEM((Z, 1, V), f32),
            pltpu.VMEM((META, W), jnp.int32),
        ),
        [pltpu.SMEM((Z,), jnp.int32), pltpu.SMEM((ROUNDS, Z), jnp.int32), pltpu.SemaphoreType.DMA((5,))],
    )(far(x), far(duals), far(cost), far(sizes), far(partners))
    ties = near(lax.all_to_all(ties, NEAR, 0, 0, tiled=True))
    block, dual, hinv = call(
        first_side_kernel,
        "first_side",
        [VMEM] * 5 + [HBM],
        (pltpu.VMEM((T * Z, BW), bf16), pltpu.VMEM((Z, TIE), f32), pltpu.VMEM((ROWS * Z, V), bf16)),
        [pltpu.SemaphoreType.DMA],
    )(meta, x, duals, cost, ties, far(hinv))
    block = near(lax.all_to_all(block, SLOTS, 0, 0, tiled=True))
    current, part = call(
        first_product_kernel,
        "first_product",
        [VMEM] * 3,
        (pltpu.VMEM((RP, T * Z), f32), pltpu.VMEM((SECOND_ROWS, T * Z), f32)),
    )(meta, block, hinv)
    two = near(lax.ppermute(part, AXES, swap_route(SECOND)))
    one = near(lax.ppermute(current, AXES, swap_route(FIRST)))
    block = call(second_product_kernel, "second_product", [VMEM] * 6, pltpu.VMEM((T * Z, DW), bf16))(
        meta, block, current, two, one, hinv
    )
    block = near(lax.all_to_all(block, SLOTS, 0, 0, tiled=True))
    shape = jax.ShapeDtypeStruct
    return call(last_sum_kernel, "last_sum", [VMEM] * 3, (shape((Z, 1, V), f32), shape((Z, 1, TIE), f32)))(
        meta, block, dual
    )


def solution(mesh):
    fine = Mesh(mesh.devices.reshape(SIZES), AXES)
    whole = P(ZONE, PERIOD, None)
    return jax.shard_map(
        shards,
        mesh=fine,
        in_specs=(whole, whole, whole, whole, P(ZONE), P(None, ZONE)),
        out_specs=(whole, whole),
        check_vma=False,
    )
```

```python
import itertools

import jax
import jax.numpy as jnp
from jax import lax
from jax.experimental import pallas as pl
from jax.experimental.pallas import tpu as pltpu
from jax.sharding import Mesh, PartitionSpec as P

V = 1600
W = 128
ROUNDS = 4
TIE = ROUNDS * W
RAMP = TIE + W
Z = 8
T = 16
ROWS = V // T
VP = 1664
LOW = 92
TAIL = 1536
RAMP_AT = V + ROWS + LOW
BW = RAMP_AT + W
RP = 104
SIZE_ROW, SIZE_LANE, MATE_ROW = 0, Z, 2 * Z
MATE_LANE = MATE_ROW + ROUNDS * Z
META = MATE_LANE + ROUNDS * Z
DW = VP + W
AXES = ("xh", "xl", "zh", "core", "y", "zl")
SIZES = (2, 2, 4, 2, 8, 2)
ZONE = ("xh", "xl", "zh", "core")
NEAR = ("xl", "zh", "core")
PERIOD = ("y", "zl")
SLOTS = ("zl", "y")
ORDER = tuple(range(0, T, 2)) + tuple(range(1, T, 2))
HALF = T * Z // 2
SECOND_ROWS = 56
FIRST = {0: 0, 1: 1, 2: 2, 3: 2, 4: 3, 5: 3}
SECOND = {1: 0, 2: 1, 3: 3}


def near_index():
    return (lax.axis_index("xl") * 4 + lax.axis_index("zh")) * 2 + lax.axis_index("core")


def period_index():
    return lax.axis_index("y") * 2 + lax.axis_index("zl")


def swap_route(rounds):
    route = []
    for place in itertools.product(*[range(size) for size in SIZES]):
        xh, xl, zh, core, y, zl = place
        k = y * 2 + zl
        if k in rounds:
            zone = ((xh * 2 + xl) * 4 + zh) * 2 + core
            mate = zone ^ (1 << rounds[k])
            there = (mate >> 4, (mate >> 3) & 1, (mate >> 1) & 3, mate & 1, y, zl)
            ends = []
            for spot in (place, there):
                flat = 0
                for size, index in zip(SIZES, spot):
                    flat = flat * size + index
                ends.append(flat)
            route.append(tuple(ends))
    return route


def rounded(values):
    return values.astype(jnp.bfloat16)


def tie_blocks_kernel(x_hbm, ties_hbm, blocks_ref, sems, out_sems):
    me = near_index()
    copies = []
    for r in range(ROUNDS):
        here = x_hbm.at[:, 0, r * W : (r + 1) * W]
        copies.append(pltpu.make_async_copy(here, blocks_ref.at[r], sems.at[r]))
        copies[-1].start()
    sends = []
    for r in range(ROUNDS):
        slot = pl.multiple_of((me ^ (1 << r)) * Z, Z)
        copies[r].wait()
        sends.append(pltpu.make_async_copy(blocks_ref.at[r], ties_hbm.at[pl.ds(slot, Z), :], out_sems.at[r]))
        sends[-1].start()
    for send in sends:
        send.wait()


def fetch_kernel(x_hbm, dual_hbm, cost_hbm, sizes_hbm, partners_hbm, hinv_hbm, x_ref, dual_ref, cost_ref, meta_ref, hinv_ref, sizes_ref, partners_ref, sems):
    pairs = (
        (sizes_hbm, sizes_ref),
        (partners_hbm, partners_ref),
        (x_hbm, x_ref),
        (dual_hbm, dual_ref),
        (cost_hbm, cost_ref),
        (hinv_hbm, hinv_ref),
    )
    copies = [pltpu.make_async_copy(here, there, sems.at[i]) for i, (here, there) in enumerate(pairs)]
    for copy in copies:
        copy.start()
    row = lax.broadcasted_iota(jnp.int32, (Z, W), 0)
    lane = lax.broadcasted_iota(jnp.int32, (Z, W), 1) & (Z - 1)
    for copy in copies[:2]:
        copy.wait()

    def spread(index, value):
        out = jnp.zeros((Z, W), jnp.int32)
        for z in range(Z):
            out = jnp.where(index == z, value(z), out)
        return out

    meta_ref[SIZE_ROW : SIZE_ROW + Z, :] = spread(row, lambda z: sizes_ref[z])
    meta_ref[SIZE_LANE : SIZE_LANE + Z, :] = spread(lane, lambda z: sizes_ref[z])
    for r in range(ROUNDS):
        at = MATE_ROW + r * Z
        meta_ref[at : at + Z, :] = spread(row, lambda z: partners_ref[r, z])
        at = MATE_LANE + r * Z
        meta_ref[at : at + Z, :] = spread(lane, lambda z: partners_ref[r, z])
    for copy in copies[2:]:
        copy.wait()


def live_rows(meta_ref):
    lane = lax.broadcasted_iota(jnp.int32, (Z, VP), 1)
    size = jnp.concatenate([meta_ref[SIZE_ROW : SIZE_ROW + Z, :]] * (VP // W), axis=1)
    return (lane < size).astype(jnp.float32)[:, :V]


def first_side_kernel(meta_ref, x_ref, dual_ref, cost_ref, ties_ref, out_ref, dual_out_ref):
    me = near_index()
    x = x_ref[:, 0, :]
    cost = cost_ref[:, 0, :]
    dual = dual_ref[:, 0, :]
    terms, new_duals = [], []
    for r in range(ROUNDS):
        own = x[:, r * W : (r + 1) * W]
        slot = (me ^ (1 << r)) * Z
        mate = meta_ref[MATE_ROW + r * Z : MATE_ROW + (r + 1) * Z, :]
        other = jnp.zeros((Z, W), jnp.float32)
        for z in range(Z):
            other = jnp.where(mate == z, ties_ref[pl.ds(slot + z, 1), :], other)
        updated = dual[:, r * W : (r + 1) * W] + 0.5 * (own - other)
        new_duals.append(updated)
        terms.append(0.5 * (own + other) - updated)
    new_dual = jnp.concatenate(new_duals, axis=1)
    rest = jnp.zeros((Z, V - TIE), jnp.float32)
    right = (0.5 * x - cost + jnp.concatenate(terms + [rest], axis=1)) * live_rows(meta_ref)
    dual_out_ref[...] = new_dual
    later = cost + jnp.concatenate([new_dual, rest], axis=1)
    later_high = rounded(later).astype(jnp.float32)
    later_low = later - later_high
    head, ramp = rounded(right[:, :TAIL]), rounded(x[:, TIE:RAMP])
    for slot, k in enumerate(ORDER):
        at = k * ROWS
        tail = [right[:, TAIL:], later_high[:, at : at + ROWS], later_low[:, at : at + LOW]]
        out_ref[slot * Z : (slot + 1) * Z, :] = jnp.concatenate(
            [head, rounded(jnp.concatenate(tail, axis=1)), ramp], axis=1
        )


def zone_match():
    row = lax.broadcasted_iota(jnp.int32, (Z, T * Z), 0)
    lane = lax.broadcasted_iota(jnp.int32, (Z, T * Z), 1)
    return row == (lane & (Z - 1))


def first_product_kernel(meta_ref, block_ref, hinv_ref, out_ref, second_ref):
    first = period_index() * ROWS
    ramp = block_ref[:, RAMP_AT:].astype(jnp.float32)
    edge = jnp.zeros((Z, W), jnp.float32)
    even, odd = ramp[:HALF], ramp[HALF:]
    around = jnp.concatenate(
        [
            odd + jnp.concatenate([edge, odd[:-Z]], axis=0),
            even + jnp.concatenate([even[Z:], edge], axis=0),
        ],
        axis=0,
    )
    ramp_side = block_ref[:, TIE:RAMP].astype(jnp.float32) + 0.5 * around
    side = jnp.concatenate([block_ref[:, :TIE], rounded(ramp_side), block_ref[:, RAMP:V]], axis=1)
    product = lax.dot_general(
        hinv_ref[...], side, (((1,), (1,)), ((), ())), preferred_element_type=jnp.float32
    ).reshape(ROWS, Z, T * Z)
    current = jnp.sum(jnp.where(zone_match()[None], product, 0.0), axis=1)
    row = lax.broadcasted_iota(jnp.int32, (ROWS, T * Z), 0) + first
    size = meta_ref[SIZE_LANE : SIZE_LANE + 1, :]
    current = jnp.where(row < size, current, 0.0)
    current = jnp.concatenate([current, jnp.zeros((RP - ROWS, T * Z), jnp.float32)], axis=0)
    out_ref[...] = current
    second_ref[...] = jnp.where(period_index() == 3, current[RP - SECOND_ROWS :], current[:SECOND_ROWS])


def second_product_kernel(meta_ref, block_ref, current_ref, two_ref, one_ref, hinv_ref, out_ref):
    k = period_index()
    first_round = jnp.where(k == 0, 0, jnp.where(k == 1, 1, jnp.where(k <= 3, 2, 3)))
    second_round = jnp.where(k == 1, 0, jnp.where(k == 2, 1, jnp.where(k == 3, 3, 0)))
    current = current_ref[...]
    later = block_ref[:, TAIL:RAMP_AT].astype(jnp.float32).T[V - TAIL :]
    blank = jnp.zeros((RP - LOW, T * Z), jnp.float32)
    later = jnp.concatenate([later[:ROWS], blank[: RP - ROWS]], axis=0) + jnp.concatenate([later[ROWS:], blank], axis=0)
    place = lax.broadcasted_iota(jnp.int32, (T * Z, T * Z), 0)
    group = lax.broadcasted_iota(jnp.int32, (T * Z, T * Z), 1) & ~(Z - 1)

    def pick(round_index):
        mate = meta_ref[pl.ds(MATE_LANE + round_index * Z, 1), :]
        return (place == group + mate).astype(jnp.float32)

    row = lax.broadcasted_iota(jnp.int32, (RP, T * Z), 0)
    lane = lax.broadcasted_iota(jnp.int32, (RP, T * Z), 1)
    entry = row + k * ROWS
    round_of = entry >> 7
    tie = entry < TIE
    blank = jnp.zeros((RP - SECOND_ROWS, T * Z), jnp.float32)
    second = jnp.where(
        k == 3,
        jnp.concatenate([blank, two_ref[...]], axis=0),
        jnp.concatenate([two_ref[...], blank], axis=0),
    )
    received = jnp.concatenate(
        [
            jnp.where(tie & (round_of == first_round), one_ref[...], 0.0),
            jnp.where(tie & (round_of == second_round) & (k >= 1) & (k <= 3), second, 0.0),
        ],
        axis=1,
    )
    picks = jnp.concatenate([pick(first_round), pick(second_round)], axis=0)
    other = jnp.dot(received, picks, preferred_element_type=jnp.float32, precision=lax.Precision.HIGHEST)
    beside = pltpu.roll(current, HALF, 1)
    before = jnp.where(lane < Z, 0.0, pltpu.roll(beside, Z, 1))
    after = jnp.where(lane >= (T - 1) * Z, 0.0, pltpu.roll(beside, (T - 1) * Z, 1))
    ramp = jnp.where((entry >= TIE) & (entry < RAMP), 0.5 * (beside + jnp.where(lane < HALF, before, after)), 0.0)
    right = 0.5 * current - later + jnp.where(tie, other, ramp)
    size = meta_ref[SIZE_LANE : SIZE_LANE + 1, :]
    right = jnp.where(entry < size, right, 0.0)[:ROWS]
    side = rounded(jnp.where(zone_match()[None], right[:, None, :], 0.0).reshape(ROWS * Z, T * Z))
    step = jnp.where(tie, 0.5 * (current - other), 0.0)
    step = jnp.concatenate([step, jnp.zeros((W - RP, T * Z), jnp.float32)], axis=0).T
    out_ref[:, VP:] = rounded(step)
    total = lax.dot_general(side, hinv_ref[...], (((0,), (0,)), ((), ())), preferred_element_type=jnp.float32)
    out_ref[:, :V] = rounded(total)
    out_ref[:, V:VP] = jnp.zeros((T * Z, VP - V), jnp.bfloat16)


def last_sum_kernel(meta_ref, block_ref, dual_ref, primal_ref, dual_out_ref):
    total = jnp.zeros((Z, V), jnp.float32)
    for k in range(T):
        total = total + block_ref[k * Z : (k + 1) * Z, :V].astype(jnp.float32)
    primal_ref[:, 0, :] = total * live_rows(meta_ref)
    steps = []
    for k in range(-(-TIE // ROWS)):
        slot = ORDER.index(k)
        part = block_ref[slot * Z : (slot + 1) * Z, VP:].astype(jnp.float32)
        steps.append(part[:, : min(ROWS, TIE - k * ROWS)])
    dual_out_ref[:, 0, :] = dual_ref[...] + jnp.concatenate(steps, axis=1)


HBM = pl.BlockSpec(memory_space=pltpu.HBM)
VMEM = pl.BlockSpec(memory_space=pltpu.VMEM)


def call(kernel, name, in_specs, out_shape, scratch=(), out_spec=VMEM):
    many = isinstance(out_shape, tuple)
    return pl.pallas_call(
        kernel,
        name=name,
        in_specs=in_specs,
        out_specs=tuple(out_spec for _ in out_shape) if many else out_spec,
        out_shape=out_shape,
        scratch_shapes=scratch,
        compiler_params=pltpu.CompilerParams(vmem_limit_bytes=16 << 20),
    )


def near(values):
    return pltpu.with_memory_space_constraint(values, pltpu.VMEM)


def far(values):
    return pltpu.with_memory_space_constraint(values, pltpu.HBM)


def shards(x, duals, cost, hinv, sizes, partners):
    f32, bf16 = jnp.float32, jnp.bfloat16
    hinv = jnp.transpose(hinv, (1, 0, 2)).reshape(ROWS * Z, V)
    ties = call(
        tie_blocks_kernel,
        "tie_blocks",
        [HBM],
        pltpu.HBM((T * Z, W), f32),
        [pltpu.VMEM((ROUNDS, Z, W), f32)] + [pltpu.SemaphoreType.DMA((ROUNDS,))] * 2,
        HBM,
    )(far(x))
    ties = near(lax.all_to_all(ties, NEAR, 0, 0, tiled=True))
    x, duals, cost, meta, hinv = call(
        fetch_kernel,
        "fetch",
        [HBM] * 6,
        (
            pltpu.VMEM((Z, 1, V), f32),
            pltpu.VMEM((Z, 1, TIE), f32),
            pltpu.VMEM((Z, 1, V), f32),
            pltpu.VMEM((META, W), jnp.int32),
            pltpu.VMEM((ROWS * Z, V), bf16),
        ),
        [pltpu.SMEM((Z,), jnp.int32), pltpu.SMEM((ROUNDS, Z), jnp.int32), pltpu.SemaphoreType.DMA((6,))],
    )(far(x), far(duals), far(cost), far(sizes), far(partners), far(hinv))
    block, dual = call(
        first_side_kernel,
        "first_side",
        [VMEM] * 5,
        (pltpu.VMEM((T * Z, BW), bf16), pltpu.VMEM((Z, TIE), f32)),
    )(meta, x, duals, cost, ties)
    block = near(lax.all_to_all(block, SLOTS, 0, 0, tiled=True))
    current, part = call(
        first_product_kernel,
        "first_product",
        [VMEM] * 3,
        (pltpu.VMEM((RP, T * Z), f32), pltpu.VMEM((SECOND_ROWS, T * Z), f32)),
    )(meta, block, hinv)
    two = near(lax.ppermute(part, AXES, swap_route(SECOND)))
    one = near(lax.ppermute(current, AXES, swap_route(FIRST)))
    block = call(second_product_kernel, "second_product", [VMEM] * 6, pltpu.VMEM((T * Z, DW), bf16))(
        meta, block, current, two, one, hinv
    )
    block = near(lax.all_to_all(block, SLOTS, 0, 0, tiled=True))
    shape = jax.ShapeDtypeStruct
    return call(last_sum_kernel, "last_sum", [VMEM] * 3, (shape((Z, 1, V), f32), shape((Z, 1, TIE), f32)))(
        meta, block, dual
    )


def solution(mesh):
    fine = Mesh(mesh.devices.reshape(SIZES), AXES)
    whole = P(ZONE, PERIOD, None)
    return jax.shard_map(
        shards,
        mesh=fine,
        in_specs=(whole, whole, whole, whole, P(ZONE), P(None, ZONE)),
        out_specs=(whole, whole),
        check_vma=False,
    )
```

```python
import itertools

import jax
import jax.numpy as jnp
from jax import lax
from jax.experimental import pallas as pl
from jax.experimental.pallas import tpu as pltpu
from jax.sharding import Mesh, PartitionSpec as P

V = 1600
W = 128
ROUNDS = 4
TIE = ROUNDS * W
RAMP = TIE + W
Z = 8
T = 16
ROWS = V // T
VP = 1664
LOW = 92
TAIL = 1536
RAMP_AT = V + ROWS + LOW
BW = RAMP_AT + W
RP = 104
SIZE_ROW, SIZE_LANE, MATE_ROW = 0, Z, 2 * Z
MATE_LANE = MATE_ROW + ROUNDS * Z
META = MATE_LANE + ROUNDS * Z
DW = VP + W
AXES = ("xh", "xl", "zh", "core", "y", "zl")
SIZES = (2, 2, 4, 2, 8, 2)
ZONE = ("xh", "xl", "zh", "core")
NEAR = ("zh", "core")
MEMBERS = 8
PERIOD = ("y", "zl")
SLOTS = ("zl", "y")
ORDER = tuple(range(0, T, 2)) + tuple(range(1, T, 2))
HALF = T * Z // 2
SECOND_ROWS = 56
FIRST = {0: 0, 1: 1, 2: 2, 3: 2, 4: 3, 5: 3}
SECOND = {1: 0, 2: 1, 3: 3}


def near_index():
    return lax.axis_index("zh") * 2 + lax.axis_index("core")


def period_index():
    return lax.axis_index("y") * 2 + lax.axis_index("zl")


def swap_route(rounds):
    route = []
    for place in itertools.product(*[range(size) for size in SIZES]):
        xh, xl, zh, core, y, zl = place
        k = y * 2 + zl
        if k in rounds:
            zone = ((xh * 2 + xl) * 4 + zh) * 2 + core
            mate = zone ^ (1 << rounds[k])
            there = (mate >> 4, (mate >> 3) & 1, (mate >> 1) & 3, mate & 1, y, zl)
            ends = []
            for spot in (place, there):
                flat = 0
                for size, index in zip(SIZES, spot):
                    flat = flat * size + index
                ends.append(flat)
            route.append(tuple(ends))
    return route


def rounded(values):
    return values.astype(jnp.bfloat16)


def tie_blocks_kernel(x_hbm, ties_hbm, last_hbm, blocks_ref, sems, out_sems):
    me = near_index()
    copies = []
    for r in range(ROUNDS):
        here = x_hbm.at[:, 0, r * W : (r + 1) * W]
        copies.append(pltpu.make_async_copy(here, blocks_ref.at[r], sems.at[r]))
        copies[-1].start()
    sends = []
    for r in range(ROUNDS):
        copies[r].wait()
        if r < ROUNDS - 1:
            there = ties_hbm.at[pl.ds(pl.multiple_of((me ^ (1 << r)) * Z, Z), Z), :]
        else:
            there = last_hbm
        sends.append(pltpu.make_async_copy(blocks_ref.at[r], there, out_sems.at[r]))
        sends[-1].start()
    for send in sends:
        send.wait()


def fetch_kernel(x_hbm, dual_hbm, cost_hbm, sizes_hbm, partners_hbm, hinv_hbm, x_ref, dual_ref, cost_ref, meta_ref, hinv_ref, sizes_ref, partners_ref, sems):
    pairs = (
        (sizes_hbm, sizes_ref),
        (partners_hbm, partners_ref),
        (x_hbm, x_ref),
        (dual_hbm, dual_ref),
        (cost_hbm, cost_ref),
        (hinv_hbm, hinv_ref),
    )
    copies = [pltpu.make_async_copy(here, there, sems.at[i]) for i, (here, there) in enumerate(pairs)]
    for copy in copies:
        copy.start()
    row = lax.broadcasted_iota(jnp.int32, (Z, W), 0)
    lane = lax.broadcasted_iota(jnp.int32, (Z, W), 1) & (Z - 1)
    for copy in copies[:2]:
        copy.wait()

    def spread(index, value):
        out = jnp.zeros((Z, W), jnp.int32)
        for z in range(Z):
            out = jnp.where(index == z, value(z), out)
        return out

    meta_ref[SIZE_ROW : SIZE_ROW + Z, :] = spread(row, lambda z: sizes_ref[z])
    meta_ref[SIZE_LANE : SIZE_LANE + Z, :] = spread(lane, lambda z: sizes_ref[z])
    for r in range(ROUNDS):
        at = MATE_ROW + r * Z
        meta_ref[at : at + Z, :] = spread(row, lambda z: partners_ref[r, z])
        at = MATE_LANE + r * Z
        meta_ref[at : at + Z, :] = spread(lane, lambda z: partners_ref[r, z])
    for copy in copies[2:]:
        copy.wait()


def live_rows(meta_ref):
    lane = lax.broadcasted_iota(jnp.int32, (Z, VP), 1)
    size = jnp.concatenate([meta_ref[SIZE_ROW : SIZE_ROW + Z, :]] * (VP // W), axis=1)
    return (lane < size).astype(jnp.float32)[:, :V]


def first_side_kernel(meta_ref, x_ref, dual_ref, cost_ref, ties_ref, last_ref, out_ref, dual_out_ref):
    me = near_index()
    x = x_ref[:, 0, :]
    cost = cost_ref[:, 0, :]
    dual = dual_ref[:, 0, :]
    terms, new_duals = [], []
    for r in range(ROUNDS):
        own = x[:, r * W : (r + 1) * W]
        slot = (me ^ (1 << r)) * Z
        mate = meta_ref[MATE_ROW + r * Z : MATE_ROW + (r + 1) * Z, :]
        other = jnp.zeros((Z, W), jnp.float32)
        for z in range(Z):
            from_z = ties_ref[pl.ds(slot + z, 1), :] if r < ROUNDS - 1 else last_ref[z : z + 1, :]
            other = jnp.where(mate == z, from_z, other)
        updated = dual[:, r * W : (r + 1) * W] + 0.5 * (own - other)
        new_duals.append(updated)
        terms.append(0.5 * (own + other) - updated)
    new_dual = jnp.concatenate(new_duals, axis=1)
    rest = jnp.zeros((Z, V - TIE), jnp.float32)
    right = (0.5 * x - cost + jnp.concatenate(terms + [rest], axis=1)) * live_rows(meta_ref)
    dual_out_ref[...] = new_dual
    later = cost + jnp.concatenate([new_dual, rest], axis=1)
    later_high = rounded(later).astype(jnp.float32)
    later_low = later - later_high
    head, ramp = rounded(right[:, :TAIL]), rounded(x[:, TIE:RAMP])
    for slot, k in enumerate(ORDER):
        at = k * ROWS
        tail = [right[:, TAIL:], later_high[:, at : at + ROWS], later_low[:, at : at + LOW]]
        out_ref[slot * Z : (slot + 1) * Z, :] = jnp.concatenate(
            [head, rounded(jnp.concatenate(tail, axis=1)), ramp], axis=1
        )


def zone_match():
    row = lax.broadcasted_iota(jnp.int32, (Z, T * Z), 0)
    lane = lax.broadcasted_iota(jnp.int32, (Z, T * Z), 1)
    return row == (lane & (Z - 1))


def first_product_kernel(meta_ref, block_ref, hinv_ref, out_ref, second_ref):
    first = period_index() * ROWS
    ramp = block_ref[:, RAMP_AT:].astype(jnp.float32)
    edge = jnp.zeros((Z, W), jnp.float32)
    even, odd = ramp[:HALF], ramp[HALF:]
    around = jnp.concatenate(
        [
            odd + jnp.concatenate([edge, odd[:-Z]], axis=0),
            even + jnp.concatenate([even[Z:], edge], axis=0),
        ],
        axis=0,
    )
    ramp_side = block_ref[:, TIE:RAMP].astype(jnp.float32) + 0.5 * around
    side = jnp.concatenate([block_ref[:, :TIE], rounded(ramp_side), block_ref[:, RAMP:V]], axis=1)
    product = lax.dot_general(
        hinv_ref[...], side, (((1,), (1,)), ((), ())), preferred_element_type=jnp.float32
    ).reshape(ROWS, Z, T * Z)
    current = jnp.sum(jnp.where(zone_match()[None], product, 0.0), axis=1)
    row = lax.broadcasted_iota(jnp.int32, (ROWS, T * Z), 0) + first
    size = meta_ref[SIZE_LANE : SIZE_LANE + 1, :]
    current = jnp.where(row < size, current, 0.0)
    current = jnp.concatenate([current, jnp.zeros((RP - ROWS, T * Z), jnp.float32)], axis=0)
    out_ref[...] = current
    second_ref[...] = jnp.where(period_index() == 3, current[RP - SECOND_ROWS :], current[:SECOND_ROWS])


def second_product_kernel(meta_ref, block_ref, current_ref, two_ref, one_ref, hinv_ref, out_ref):
    k = period_index()
    first_round = jnp.where(k == 0, 0, jnp.where(k == 1, 1, jnp.where(k <= 3, 2, 3)))
    second_round = jnp.where(k == 1, 0, jnp.where(k == 2, 1, jnp.where(k == 3, 3, 0)))
    current = current_ref[...]
    later = block_ref[:, TAIL:RAMP_AT].astype(jnp.float32).T[V - TAIL :]
    blank = jnp.zeros((RP - LOW, T * Z), jnp.float32)
    later = jnp.concatenate([later[:ROWS], blank[: RP - ROWS]], axis=0) + jnp.concatenate([later[ROWS:], blank], axis=0)
    place = lax.broadcasted_iota(jnp.int32, (T * Z, T * Z), 0)
    group = lax.broadcasted_iota(jnp.int32, (T * Z, T * Z), 1) & ~(Z - 1)

    def pick(round_index):
        mate = meta_ref[pl.ds(MATE_LANE + round_index * Z, 1), :]
        return (place == group + mate).astype(jnp.float32)

    row = lax.broadcasted_iota(jnp.int32, (RP, T * Z), 0)
    lane = lax.broadcasted_iota(jnp.int32, (RP, T * Z), 1)
    entry = row + k * ROWS
    round_of = entry >> 7
    tie = entry < TIE
    blank = jnp.zeros((RP - SECOND_ROWS, T * Z), jnp.float32)
    second = jnp.where(
        k == 3,
        jnp.concatenate([blank, two_ref[...]], axis=0),
        jnp.concatenate([two_ref[...], blank], axis=0),
    )
    received = jnp.concatenate(
        [
            jnp.where(tie & (round_of == first_round), one_ref[...], 0.0),
            jnp.where(tie & (round_of == second_round) & (k >= 1) & (k <= 3), second, 0.0),
        ],
        axis=1,
    )
    picks = jnp.concatenate([pick(first_round), pick(second_round)], axis=0)
    other = jnp.dot(received, picks, preferred_element_type=jnp.float32, precision=lax.Precision.HIGHEST)
    beside = pltpu.roll(current, HALF, 1)
    before = jnp.where(lane < Z, 0.0, pltpu.roll(beside, Z, 1))
    after = jnp.where(lane >= (T - 1) * Z, 0.0, pltpu.roll(beside, (T - 1) * Z, 1))
    ramp = jnp.where((entry >= TIE) & (entry < RAMP), 0.5 * (beside + jnp.where(lane < HALF, before, after)), 0.0)
    right = 0.5 * current - later + jnp.where(tie, other, ramp)
    size = meta_ref[SIZE_LANE : SIZE_LANE + 1, :]
    right = jnp.where(entry < size, right, 0.0)[:ROWS]
    side = rounded(jnp.where(zone_match()[None], right[:, None, :], 0.0).reshape(ROWS * Z, T * Z))
    step = jnp.where(tie, 0.5 * (current - other), 0.0)
    step = jnp.concatenate([step, jnp.zeros((W - RP, T * Z), jnp.float32)], axis=0).T
    out_ref[:, VP:] = rounded(step)
    total = lax.dot_general(side, hinv_ref[...], (((0,), (0,)), ((), ())), preferred_element_type=jnp.float32)
    out_ref[:, :V] = rounded(total)
    out_ref[:, V:VP] = jnp.zeros((T * Z, VP - V), jnp.bfloat16)


def last_sum_kernel(meta_ref, block_ref, dual_ref, primal_ref, dual_out_ref):
    total = jnp.zeros((Z, V), jnp.float32)
    for k in range(T):
        total = total + block_ref[k * Z : (k + 1) * Z, :V].astype(jnp.float32)
    primal_ref[:, 0, :] = total * live_rows(meta_ref)
    steps = []
    for k in range(-(-TIE // ROWS)):
        slot = ORDER.index(k)
        part = block_ref[slot * Z : (slot + 1) * Z, VP:].astype(jnp.float32)
        steps.append(part[:, : min(ROWS, TIE - k * ROWS)])
    dual_out_ref[:, 0, :] = dual_ref[...] + jnp.concatenate(steps, axis=1)


HBM = pl.BlockSpec(memory_space=pltpu.HBM)
VMEM = pl.BlockSpec(memory_space=pltpu.VMEM)


def call(kernel, name, in_specs, out_shape, scratch=(), out_spec=VMEM):
    many = isinstance(out_shape, tuple)
    return pl.pallas_call(
        kernel,
        name=name,
        in_specs=in_specs,
        out_specs=tuple(out_spec for _ in out_shape) if many else out_spec,
        out_shape=out_shape,
        scratch_shapes=scratch,
        compiler_params=pltpu.CompilerParams(vmem_limit_bytes=16 << 20),
    )


def near(values):
    return pltpu.with_memory_space_constraint(values, pltpu.VMEM)


def far(values):
    return pltpu.with_memory_space_constraint(values, pltpu.HBM)


def shards(x, duals, cost, hinv, sizes, partners):
    f32, bf16 = jnp.float32, jnp.bfloat16
    hinv = jnp.transpose(hinv, (1, 0, 2)).reshape(ROWS * Z, V)
    ties, last = call(
        tie_blocks_kernel,
        "tie_blocks",
        [HBM],
        (pltpu.HBM((MEMBERS * Z, W), f32), pltpu.HBM((Z, W), f32)),
        [pltpu.VMEM((ROUNDS, Z, W), f32)] + [pltpu.SemaphoreType.DMA((ROUNDS,))] * 2,
        HBM,
    )(far(x))
    ties = near(lax.all_to_all(ties, NEAR, 0, 0, tiled=True))
    last = near(lax.ppermute(last, "xl", [(0, 1), (1, 0)]))
    x, duals, cost, meta, hinv = call(
        fetch_kernel,
        "fetch",
        [HBM] * 6,
        (
            pltpu.VMEM((Z, 1, V), f32),
            pltpu.VMEM((Z, 1, TIE), f32),
            pltpu.VMEM((Z, 1, V), f32),
            pltpu.VMEM((META, W), jnp.int32),
            pltpu.VMEM((ROWS * Z, V), bf16),
        ),
        [pltpu.SMEM((Z,), jnp.int32), pltpu.SMEM((ROUNDS, Z), jnp.int32), pltpu.SemaphoreType.DMA((6,))],
    )(far(x), far(duals), far(cost), far(sizes), far(partners), far(hinv))
    block, dual = call(
        first_side_kernel,
        "first_side",
        [VMEM] * 6,
        (pltpu.VMEM((T * Z, BW), bf16), pltpu.VMEM((Z, TIE), f32)),
    )(meta, x, duals, cost, ties, last)
    block = near(lax.all_to_all(block, SLOTS, 0, 0, tiled=True))
    current, part = call(
        first_product_kernel,
        "first_product",
        [VMEM] * 3,
        (pltpu.VMEM((RP, T * Z), f32), pltpu.VMEM((SECOND_ROWS, T * Z), f32)),
    )(meta, block, hinv)
    two = near(lax.ppermute(part, AXES, swap_route(SECOND)))
    one = near(lax.ppermute(current, AXES, swap_route(FIRST)))
    block = call(second_product_kernel, "second_product", [VMEM] * 6, pltpu.VMEM((T * Z, DW), bf16))(
        meta, block, current, two, one, hinv
    )
    block = near(lax.all_to_all(block, SLOTS, 0, 0, tiled=True))
    shape = jax.ShapeDtypeStruct
    return call(last_sum_kernel, "last_sum", [VMEM] * 3, (shape((Z, 1, V), f32), shape((Z, 1, TIE), f32)))(
        meta, block, dual
    )


def solution(mesh):
    fine = Mesh(mesh.devices.reshape(SIZES), AXES)
    whole = P(ZONE, PERIOD, None)
    return jax.shard_map(
        shards,
        mesh=fine,
        in_specs=(whole, whole, whole, whole, P(ZONE), P(None, ZONE)),
        out_specs=(whole, whole),
        check_vma=False,
    )
```

```python
import itertools

import jax
import jax.numpy as jnp
from jax import lax
from jax.experimental import pallas as pl
from jax.experimental.pallas import tpu as pltpu
from jax.sharding import Mesh, PartitionSpec as P

V = 1600
W = 128
ROUNDS = 4
TIE = ROUNDS * W
RAMP = TIE + W
Z = 8
T = 16
ROWS = V // T
VP = 1664
LOW = 92
TAIL = 1536
RAMP_AT = V + ROWS + LOW
BW = RAMP_AT + W
RP = 104
SIZE_ROW, SIZE_LANE, MATE_ROW = 0, Z, 2 * Z
MATE_LANE = MATE_ROW + ROUNDS * Z
META = MATE_LANE + ROUNDS * Z
DW = VP + W
AXES = ("xh", "xl", "zh", "core", "y", "zl")
SIZES = (2, 2, 4, 2, 8, 2)
ZONE = ("xh", "xl", "zh", "core")
NEAR = ("zh", "core")
MEMBERS = 8
PERIOD = ("y", "zl")
SLOTS = ("zl", "y")
ORDER = tuple(range(0, T, 2)) + tuple(range(1, T, 2))
HALF = T * Z // 2
SECOND_ROWS = 56
FIRST = {0: 0, 1: 1, 2: 2, 3: 2, 4: 3, 5: 3}
SECOND = {1: 0, 2: 1, 3: 3}


def near_index():
    return lax.axis_index("zh") * 2 + lax.axis_index("core")


def period_index():
    return lax.axis_index("y") * 2 + lax.axis_index("zl")


def swap_route(rounds):
    route = []
    for place in itertools.product(*[range(size) for size in SIZES]):
        xh, xl, zh, core, y, zl = place
        k = y * 2 + zl
        if k in rounds:
            zone = ((xh * 2 + xl) * 4 + zh) * 2 + core
            mate = zone ^ (1 << rounds[k])
            there = (mate >> 4, (mate >> 3) & 1, (mate >> 1) & 3, mate & 1, y, zl)
            ends = []
            for spot in (place, there):
                flat = 0
                for size, index in zip(SIZES, spot):
                    flat = flat * size + index
                ends.append(flat)
            route.append(tuple(ends))
    return route


def rounded(values):
    return values.astype(jnp.bfloat16)


def tie_blocks_kernel(x_hbm, ties_hbm, last_hbm, blocks_ref, sems, out_sems):
    me = near_index()
    copies = []
    for r in range(ROUNDS):
        here = x_hbm.at[:, 0, r * W : (r + 1) * W]
        copies.append(pltpu.make_async_copy(here, blocks_ref.at[r], sems.at[r]))
        copies[-1].start()
    sends = []
    for r in range(ROUNDS):
        copies[r].wait()
        if r < ROUNDS - 1:
            there = ties_hbm.at[pl.ds(pl.multiple_of((me ^ (1 << r)) * Z, Z), Z), :]
        else:
            there = last_hbm
        sends.append(pltpu.make_async_copy(blocks_ref.at[r], there, out_sems.at[r]))
        sends[-1].start()
    for send in sends:
        send.wait()


def fetch_kernel(x_hbm, dual_hbm, cost_hbm, sizes_hbm, partners_hbm, hinv_hbm, x_ref, dual_ref, cost_ref, meta_ref, hinv_ref, sizes_ref, partners_ref, sems):
    pairs = (
        (sizes_hbm, sizes_ref),
        (partners_hbm, partners_ref),
        (x_hbm, x_ref),
        (dual_hbm, dual_ref),
        (cost_hbm, cost_ref),
        (hinv_hbm, hinv_ref),
    )
    copies = [pltpu.make_async_copy(here, there, sems.at[i]) for i, (here, there) in enumerate(pairs)]
    for copy in copies:
        copy.start()
    row = lax.broadcasted_iota(jnp.int32, (Z, W), 0)
    lane = lax.broadcasted_iota(jnp.int32, (Z, W), 1) & (Z - 1)
    for copy in copies[:2]:
        copy.wait()

    def spread(index, value):
        out = jnp.zeros((Z, W), jnp.int32)
        for z in range(Z):
            out = jnp.where(index == z, value(z), out)
        return out

    meta_ref[SIZE_ROW : SIZE_ROW + Z, :] = spread(row, lambda z: sizes_ref[z])
    meta_ref[SIZE_LANE : SIZE_LANE + Z, :] = spread(lane, lambda z: sizes_ref[z])
    for r in range(ROUNDS):
        at = MATE_ROW + r * Z
        meta_ref[at : at + Z, :] = spread(row, lambda z: partners_ref[r, z])
        at = MATE_LANE + r * Z
        meta_ref[at : at + Z, :] = spread(lane, lambda z: partners_ref[r, z])
    for copy in copies[2:]:
        copy.wait()


def live_rows(meta_ref):
    lane = lax.broadcasted_iota(jnp.int32, (Z, VP), 1)
    size = jnp.concatenate([meta_ref[SIZE_ROW : SIZE_ROW + Z, :]] * (VP // W), axis=1)
    return (lane < size).astype(jnp.float32)[:, :V]


def first_side_kernel(meta_ref, x_ref, dual_ref, cost_ref, ties_ref, last_ref, out_ref, dual_out_ref):
    me = near_index()
    x = x_ref[:, 0, :]
    cost = cost_ref[:, 0, :]
    dual = dual_ref[:, 0, :]
    terms, new_duals = [], []
    for r in range(ROUNDS):
        own = x[:, r * W : (r + 1) * W]
        slot = (me ^ (1 << r)) * Z
        mate = meta_ref[MATE_ROW + r * Z : MATE_ROW + (r + 1) * Z, :]
        other = jnp.zeros((Z, W), jnp.float32)
        for z in range(Z):
            from_z = ties_ref[pl.ds(slot + z, 1), :] if r < ROUNDS - 1 else last_ref[z : z + 1, :]
            other = jnp.where(mate == z, from_z, other)
        updated = dual[:, r * W : (r + 1) * W] + 0.5 * (own - other)
        new_duals.append(updated)
        terms.append(0.5 * (own + other) - updated)
    new_dual = jnp.concatenate(new_duals, axis=1)
    rest = jnp.zeros((Z, V - TIE), jnp.float32)
    right = (0.5 * x - cost + jnp.concatenate(terms + [rest], axis=1)) * live_rows(meta_ref)
    dual_out_ref[...] = new_dual
    later = cost + jnp.concatenate([new_dual, rest], axis=1)
    later_high = rounded(later).astype(jnp.float32)
    later_low = later - later_high
    head, ramp = rounded(right[:, :TAIL]), rounded(x[:, TIE:RAMP])
    for slot, k in enumerate(ORDER):
        at = k * ROWS
        tail = [right[:, TAIL:], later_high[:, at : at + ROWS], later_low[:, at : at + LOW]]
        out_ref[slot * Z : (slot + 1) * Z, :] = jnp.concatenate(
            [head, rounded(jnp.concatenate(tail, axis=1)), ramp], axis=1
        )


def zone_match():
    row = lax.broadcasted_iota(jnp.int32, (Z, T * Z), 0)
    lane = lax.broadcasted_iota(jnp.int32, (Z, T * Z), 1)
    return row == (lane & (Z - 1))


def first_product_kernel(meta_ref, block_ref, hinv_ref, out_ref, second_ref):
    first = period_index() * ROWS
    ramp = block_ref[:, RAMP_AT:].astype(jnp.float32)
    edge = jnp.zeros((Z, W), jnp.float32)
    even, odd = ramp[:HALF], ramp[HALF:]
    around = jnp.concatenate(
        [
            odd + jnp.concatenate([edge, odd[:-Z]], axis=0),
            even + jnp.concatenate([even[Z:], edge], axis=0),
        ],
        axis=0,
    )
    ramp_side = block_ref[:, TIE:RAMP].astype(jnp.float32) + 0.5 * around
    side = jnp.concatenate([block_ref[:, :TIE], rounded(ramp_side), block_ref[:, RAMP:V]], axis=1)
    product = lax.dot_general(
        hinv_ref[...], side, (((1,), (1,)), ((), ())), preferred_element_type=jnp.float32
    ).reshape(ROWS, Z, T * Z)
    current = jnp.sum(jnp.where(zone_match()[None], product, 0.0), axis=1)
    row = lax.broadcasted_iota(jnp.int32, (ROWS, T * Z), 0) + first
    size = meta_ref[SIZE_LANE : SIZE_LANE + 1, :]
    current = jnp.where(row < size, current, 0.0)
    current = jnp.concatenate([current, jnp.zeros((RP - ROWS, T * Z), jnp.float32)], axis=0)
    out_ref[...] = current
    second_ref[...] = jnp.where(period_index() == 3, current[RP - SECOND_ROWS :], current[:SECOND_ROWS])


def rounds_here(k):
    first_round = jnp.where(k == 0, 0, jnp.where(k == 1, 1, jnp.where(k <= 3, 2, 3)))
    second_round = jnp.where(k == 1, 0, jnp.where(k == 2, 1, jnp.where(k == 3, 3, 0)))
    return first_round, second_round


def second_side_kernel(meta_ref, block_ref, current_ref, side_ref, picks_ref):
    k = period_index()
    current = current_ref[...]
    later = block_ref[:, TAIL:RAMP_AT].astype(jnp.float32).T[V - TAIL :]
    blank = jnp.zeros((RP - LOW, T * Z), jnp.float32)
    later = jnp.concatenate([later[:ROWS], blank[: RP - ROWS]], axis=0) + jnp.concatenate([later[ROWS:], blank], axis=0)
    place = lax.broadcasted_iota(jnp.int32, (T * Z, T * Z), 0)
    group = lax.broadcasted_iota(jnp.int32, (T * Z, T * Z), 1) & ~(Z - 1)
    for i, round_index in enumerate(rounds_here(k)):
        mate = meta_ref[pl.ds(MATE_LANE + round_index * Z, 1), :]
        picks_ref[i * T * Z : (i + 1) * T * Z, :] = (place == group + mate).astype(jnp.float32)
    lane = lax.broadcasted_iota(jnp.int32, (RP, T * Z), 1)
    entry = lax.broadcasted_iota(jnp.int32, (RP, T * Z), 0) + k * ROWS
    beside = pltpu.roll(current, HALF, 1)
    before = jnp.where(lane < Z, 0.0, pltpu.roll(beside, Z, 1))
    after = jnp.where(lane >= (T - 1) * Z, 0.0, pltpu.roll(beside, (T - 1) * Z, 1))
    ramp = jnp.where((entry >= TIE) & (entry < RAMP), 0.5 * (beside + jnp.where(lane < HALF, before, after)), 0.0)
    side_ref[...] = 0.5 * current - later + ramp


def second_product_kernel(meta_ref, side_ref, picks_ref, current_ref, two_ref, one_ref, hinv_ref, out_ref):
    k = period_index()
    first_round, second_round = rounds_here(k)
    current = current_ref[...]
    entry = lax.broadcasted_iota(jnp.int32, (RP, T * Z), 0) + k * ROWS
    round_of = entry >> 7
    tie = entry < TIE
    blank = jnp.zeros((RP - SECOND_ROWS, T * Z), jnp.float32)
    second = jnp.where(
        k == 3,
        jnp.concatenate([blank, two_ref[...]], axis=0),
        jnp.concatenate([two_ref[...], blank], axis=0),
    )
    received = jnp.concatenate(
        [
            jnp.where(tie & (round_of == first_round), one_ref[...], 0.0),
            jnp.where(tie & (round_of == second_round) & (k >= 1) & (k <= 3), second, 0.0),
        ],
        axis=1,
    )
    other = jnp.dot(received, picks_ref[...], preferred_element_type=jnp.float32, precision=lax.Precision.HIGHEST)
    size = meta_ref[SIZE_LANE : SIZE_LANE + 1, :]
    right = jnp.where(entry < size, side_ref[...] + other, 0.0)[:ROWS]
    side = rounded(jnp.where(zone_match()[None], right[:, None, :], 0.0).reshape(ROWS * Z, T * Z))
    step = jnp.where(tie, 0.5 * (current - other), 0.0)
    step = jnp.concatenate([step, jnp.zeros((W - RP, T * Z), jnp.float32)], axis=0).T
    out_ref[:, VP:] = rounded(step)
    total = lax.dot_general(side, hinv_ref[...], (((0,), (0,)), ((), ())), preferred_element_type=jnp.float32)
    out_ref[:, :V] = rounded(total)
    out_ref[:, V:VP] = jnp.zeros((T * Z, VP - V), jnp.bfloat16)


def last_sum_kernel(meta_ref, block_ref, dual_ref, primal_ref, dual_out_ref):
    total = jnp.zeros((Z, V), jnp.float32)
    for k in range(T):
        total = total + block_ref[k * Z : (k + 1) * Z, :V].astype(jnp.float32)
    primal_ref[:, 0, :] = total * live_rows(meta_ref)
    steps = []
    for k in range(-(-TIE // ROWS)):
        slot = ORDER.index(k)
        part = block_ref[slot * Z : (slot + 1) * Z, VP:].astype(jnp.float32)
        steps.append(part[:, : min(ROWS, TIE - k * ROWS)])
    dual_out_ref[:, 0, :] = dual_ref[...] + jnp.concatenate(steps, axis=1)


HBM = pl.BlockSpec(memory_space=pltpu.HBM)
VMEM = pl.BlockSpec(memory_space=pltpu.VMEM)


def call(kernel, name, in_specs, out_shape, scratch=(), out_spec=VMEM):
    many = isinstance(out_shape, tuple)
    return pl.pallas_call(
        kernel,
        name=name,
        in_specs=in_specs,
        out_specs=tuple(out_spec for _ in out_shape) if many else out_spec,
        out_shape=out_shape,
        scratch_shapes=scratch,
        compiler_params=pltpu.CompilerParams(vmem_limit_bytes=16 << 20),
    )


def near(values):
    return pltpu.with_memory_space_constraint(values, pltpu.VMEM)


def far(values):
    return pltpu.with_memory_space_constraint(values, pltpu.HBM)


def shards(x, duals, cost, hinv, sizes, partners):
    f32, bf16 = jnp.float32, jnp.bfloat16
    hinv = jnp.transpose(hinv, (1, 0, 2)).reshape(ROWS * Z, V)
    ties, last = call(
        tie_blocks_kernel,
        "tie_blocks",
        [HBM],
        (pltpu.HBM((MEMBERS * Z, W), f32), pltpu.HBM((Z, W), f32)),
        [pltpu.VMEM((ROUNDS, Z, W), f32)] + [pltpu.SemaphoreType.DMA((ROUNDS,))] * 2,
        HBM,
    )(far(x))
    ties = near(lax.all_to_all(ties, NEAR, 0, 0, tiled=True))
    last = near(lax.ppermute(last, "xl", [(0, 1), (1, 0)]))
    x, duals, cost, meta, hinv = call(
        fetch_kernel,
        "fetch",
        [HBM] * 6,
        (
            pltpu.VMEM((Z, 1, V), f32),
            pltpu.VMEM((Z, 1, TIE), f32),
            pltpu.VMEM((Z, 1, V), f32),
            pltpu.VMEM((META, W), jnp.int32),
            pltpu.VMEM((ROWS * Z, V), bf16),
        ),
        [pltpu.SMEM((Z,), jnp.int32), pltpu.SMEM((ROUNDS, Z), jnp.int32), pltpu.SemaphoreType.DMA((6,))],
    )(far(x), far(duals), far(cost), far(sizes), far(partners), far(hinv))
    block, dual = call(
        first_side_kernel,
        "first_side",
        [VMEM] * 6,
        (pltpu.VMEM((T * Z, BW), bf16), pltpu.VMEM((Z, TIE), f32)),
    )(meta, x, duals, cost, ties, last)
    block = near(lax.all_to_all(block, SLOTS, 0, 0, tiled=True))
    current, part = call(
        first_product_kernel,
        "first_product",
        [VMEM] * 3,
        (pltpu.VMEM((RP, T * Z), f32), pltpu.VMEM((SECOND_ROWS, T * Z), f32)),
    )(meta, block, hinv)
    two = near(lax.ppermute(part, AXES, swap_route(SECOND)))
    one = near(lax.ppermute(current, AXES, swap_route(FIRST)))
    side, picks = call(
        second_side_kernel,
        "second_side",
        [VMEM] * 3,
        (pltpu.VMEM((RP, T * Z), f32), pltpu.VMEM((2 * T * Z, T * Z), f32)),
    )(meta, block, current)
    block = call(second_product_kernel, "second_product", [VMEM] * 7, pltpu.VMEM((T * Z, DW), bf16))(
        meta, side, picks, current, two, one, hinv
    )
    block = near(lax.all_to_all(block, SLOTS, 0, 0, tiled=True))
    shape = jax.ShapeDtypeStruct
    return call(last_sum_kernel, "last_sum", [VMEM] * 3, (shape((Z, 1, V), f32), shape((Z, 1, TIE), f32)))(
        meta, block, dual
    )


def solution(mesh):
    fine = Mesh(mesh.devices.reshape(SIZES), AXES)
    whole = P(ZONE, PERIOD, None)
    return jax.shard_map(
        shards,
        mesh=fine,
        in_specs=(whole, whole, whole, whole, P(ZONE), P(None, ZONE)),
        out_specs=(whole, whole),
        check_vma=False,
    )
```

```python
import itertools

import jax
import jax.numpy as jnp
from jax import lax
from jax.experimental import pallas as pl
from jax.experimental.pallas import tpu as pltpu
from jax.sharding import Mesh, PartitionSpec as P

V = 1600
W = 128
ROUNDS = 4
TIE = ROUNDS * W
RAMP = TIE + W
Z = 8
T = 16
ROWS = V // T
VP = 1664
LOW = 92
TAIL = 1536
RAMP_AT = V + ROWS + LOW
BW = RAMP_AT + W
RP = 104
SIZE_ROW, SIZE_LANE, MATE_ROW = 0, Z, 2 * Z
MATE_LANE = MATE_ROW + ROUNDS * Z
META = MATE_LANE + ROUNDS * Z
DW = VP + W
AXES = ("xh", "xl", "zh", "core", "y", "zl")
SIZES = (2, 2, 4, 2, 8, 2)
ZONE = ("xh", "xl", "zh", "core")
NEAR = ("core", "zh")
MEMBERS = 8
FLIP = (4, 1, 2, 0)
PERIOD = ("y", "zl")
SLOTS = ("zl", "y")
ORDER = tuple(range(0, T, 2)) + tuple(range(1, T, 2))
HALF = T * Z // 2
SECOND_ROWS = 56
FIRST = {0: 0, 1: 1, 2: 2, 3: 2, 4: 3, 5: 3}
SECOND = {1: 0, 2: 1, 3: 3}


def near_index():
    return lax.axis_index("core") * 4 + lax.axis_index("zh")


def period_index():
    return lax.axis_index("y") * 2 + lax.axis_index("zl")


def swap_route(rounds):
    route = []
    for place in itertools.product(*[range(size) for size in SIZES]):
        xh, xl, zh, core, y, zl = place
        k = y * 2 + zl
        if k in rounds:
            zone = ((xh * 2 + xl) * 4 + zh) * 2 + core
            mate = zone ^ (1 << rounds[k])
            there = (mate >> 4, (mate >> 3) & 1, (mate >> 1) & 3, mate & 1, y, zl)
            ends = []
            for spot in (place, there):
                flat = 0
                for size, index in zip(SIZES, spot):
                    flat = flat * size + index
                ends.append(flat)
            route.append(tuple(ends))
    return route


def rounded(values):
    return values.astype(jnp.bfloat16)


def tie_blocks_kernel(x_hbm, ties_hbm, last_hbm, blocks_ref, sems, out_sems):
    me = near_index()
    copies = []
    for r in range(ROUNDS):
        here = x_hbm.at[:, 0, r * W : (r + 1) * W]
        copies.append(pltpu.make_async_copy(here, blocks_ref.at[r], sems.at[r]))
        copies[-1].start()
    sends = []
    for r in range(ROUNDS):
        copies[r].wait()
        if r < ROUNDS - 1:
            there = ties_hbm.at[pl.ds(pl.multiple_of((me ^ FLIP[r]) * Z, Z), Z), :]
        else:
            there = last_hbm
        sends.append(pltpu.make_async_copy(blocks_ref.at[r], there, out_sems.at[r]))
        sends[-1].start()
    for send in sends:
        send.wait()


def fetch_kernel(x_hbm, dual_hbm, cost_hbm, sizes_hbm, partners_hbm, hinv_hbm, x_ref, dual_ref, cost_ref, meta_ref, hinv_ref, sizes_ref, partners_ref, sems):
    pairs = (
        (sizes_hbm, sizes_ref),
        (partners_hbm, partners_ref),
        (x_hbm, x_ref),
        (dual_hbm, dual_ref),
        (cost_hbm, cost_ref),
        (hinv_hbm, hinv_ref),
    )
    copies = [pltpu.make_async_copy(here, there, sems.at[i]) for i, (here, there) in enumerate(pairs)]
    for copy in copies:
        copy.start()
    row = lax.broadcasted_iota(jnp.int32, (Z, W), 0)
    lane = lax.broadcasted_iota(jnp.int32, (Z, W), 1) & (Z - 1)
    for copy in copies[:2]:
        copy.wait()

    def spread(index, value):
        out = jnp.zeros((Z, W), jnp.int32)
        for z in range(Z):
            out = jnp.where(index == z, value(z), out)
        return out

    meta_ref[SIZE_ROW : SIZE_ROW + Z, :] = spread(row, lambda z: sizes_ref[z])
    meta_ref[SIZE_LANE : SIZE_LANE + Z, :] = spread(lane, lambda z: sizes_ref[z])
    for r in range(ROUNDS):
        at = MATE_ROW + r * Z
        meta_ref[at : at + Z, :] = spread(row, lambda z: partners_ref[r, z])
        at = MATE_LANE + r * Z
        meta_ref[at : at + Z, :] = spread(lane, lambda z: partners_ref[r, z])
    for copy in copies[2:]:
        copy.wait()


def live_rows(meta_ref):
    lane = lax.broadcasted_iota(jnp.int32, (Z, VP), 1)
    size = jnp.concatenate([meta_ref[SIZE_ROW : SIZE_ROW + Z, :]] * (VP // W), axis=1)
    return (lane < size).astype(jnp.float32)[:, :V]


def first_side_kernel(meta_ref, x_ref, dual_ref, cost_ref, ties_ref, last_ref, out_ref, dual_out_ref):
    me = near_index()
    x = x_ref[:, 0, :]
    cost = cost_ref[:, 0, :]
    dual = dual_ref[:, 0, :]
    terms, new_duals = [], []
    for r in range(ROUNDS):
        own = x[:, r * W : (r + 1) * W]
        slot = (me ^ FLIP[r]) * Z
        mate = meta_ref[MATE_ROW + r * Z : MATE_ROW + (r + 1) * Z, :]
        other = jnp.zeros((Z, W), jnp.float32)
        for z in range(Z):
            from_z = ties_ref[pl.ds(slot + z, 1), :] if r < ROUNDS - 1 else last_ref[z : z + 1, :]
            other = jnp.where(mate == z, from_z, other)
        updated = dual[:, r * W : (r + 1) * W] + 0.5 * (own - other)
        new_duals.append(updated)
        terms.append(0.5 * (own + other) - updated)
    new_dual = jnp.concatenate(new_duals, axis=1)
    rest = jnp.zeros((Z, V - TIE), jnp.float32)
    right = (0.5 * x - cost + jnp.concatenate(terms + [rest], axis=1)) * live_rows(meta_ref)
    dual_out_ref[...] = new_dual
    later = cost + jnp.concatenate([new_dual, rest], axis=1)
    later_high = rounded(later).astype(jnp.float32)
    later_low = later - later_high
    head, ramp = rounded(right[:, :TAIL]), rounded(x[:, TIE:RAMP])
    for slot, k in enumerate(ORDER):
        at = k * ROWS
        tail = [right[:, TAIL:], later_high[:, at : at + ROWS], later_low[:, at : at + LOW]]
        out_ref[slot * Z : (slot + 1) * Z, :] = jnp.concatenate(
            [head, rounded(jnp.concatenate(tail, axis=1)), ramp], axis=1
        )


def zone_match():
    row = lax.broadcasted_iota(jnp.int32, (Z, T * Z), 0)
    lane = lax.broadcasted_iota(jnp.int32, (Z, T * Z), 1)
    return row == (lane & (Z - 1))


def first_product_kernel(meta_ref, block_ref, hinv_ref, out_ref, second_ref):
    first = period_index() * ROWS
    ramp = block_ref[:, RAMP_AT:].astype(jnp.float32)
    edge = jnp.zeros((Z, W), jnp.float32)
    even, odd = ramp[:HALF], ramp[HALF:]
    around = jnp.concatenate(
        [
            odd + jnp.concatenate([edge, odd[:-Z]], axis=0),
            even + jnp.concatenate([even[Z:], edge], axis=0),
        ],
        axis=0,
    )
    ramp_side = block_ref[:, TIE:RAMP].astype(jnp.float32) + 0.5 * around
    side = jnp.concatenate([block_ref[:, :TIE], rounded(ramp_side), block_ref[:, RAMP:V]], axis=1)
    product = lax.dot_general(
        hinv_ref[...], side, (((1,), (1,)), ((), ())), preferred_element_type=jnp.float32
    ).reshape(ROWS, Z, T * Z)
    current = jnp.sum(jnp.where(zone_match()[None], product, 0.0), axis=1)
    row = lax.broadcasted_iota(jnp.int32, (ROWS, T * Z), 0) + first
    size = meta_ref[SIZE_LANE : SIZE_LANE + 1, :]
    current = jnp.where(row < size, current, 0.0)
    current = jnp.concatenate([current, jnp.zeros((RP - ROWS, T * Z), jnp.float32)], axis=0)
    out_ref[...] = current
    second_ref[...] = jnp.where(period_index() == 3, current[RP - SECOND_ROWS :], current[:SECOND_ROWS])


def second_product_kernel(meta_ref, block_ref, current_ref, two_ref, one_ref, hinv_ref, out_ref):
    k = period_index()
    first_round = jnp.where(k == 0, 0, jnp.where(k == 1, 1, jnp.where(k <= 3, 2, 3)))
    second_round = jnp.where(k == 1, 0, jnp.where(k == 2, 1, jnp.where(k == 3, 3, 0)))
    current = current_ref[...]
    later = block_ref[:, TAIL:RAMP_AT].astype(jnp.float32).T[V - TAIL :]
    blank = jnp.zeros((RP - LOW, T * Z), jnp.float32)
    later = jnp.concatenate([later[:ROWS], blank[: RP - ROWS]], axis=0) + jnp.concatenate([later[ROWS:], blank], axis=0)
    place = lax.broadcasted_iota(jnp.int32, (T * Z, T * Z), 0)
    group = lax.broadcasted_iota(jnp.int32, (T * Z, T * Z), 1) & ~(Z - 1)

    def pick(round_index):
        mate = meta_ref[pl.ds(MATE_LANE + round_index * Z, 1), :]
        return (place == group + mate).astype(jnp.float32)

    row = lax.broadcasted_iota(jnp.int32, (RP, T * Z), 0)
    lane = lax.broadcasted_iota(jnp.int32, (RP, T * Z), 1)
    entry = row + k * ROWS
    round_of = entry >> 7
    tie = entry < TIE
    blank = jnp.zeros((RP - SECOND_ROWS, T * Z), jnp.float32)
    second = jnp.where(
        k == 3,
        jnp.concatenate([blank, two_ref[...]], axis=0),
        jnp.concatenate([two_ref[...], blank], axis=0),
    )
    received = jnp.concatenate(
        [
            jnp.where(tie & (round_of == first_round), one_ref[...], 0.0),
            jnp.where(tie & (round_of == second_round) & (k >= 1) & (k <= 3), second, 0.0),
        ],
        axis=1,
    )
    picks = jnp.concatenate([pick(first_round), pick(second_round)], axis=0)
    other = jnp.dot(received, picks, preferred_element_type=jnp.float32, precision=lax.Precision.HIGHEST)
    beside = pltpu.roll(current, HALF, 1)
    before = jnp.where(lane < Z, 0.0, pltpu.roll(beside, Z, 1))
    after = jnp.where(lane >= (T - 1) * Z, 0.0, pltpu.roll(beside, (T - 1) * Z, 1))
    ramp = jnp.where((entry >= TIE) & (entry < RAMP), 0.5 * (beside + jnp.where(lane < HALF, before, after)), 0.0)
    right = 0.5 * current - later + jnp.where(tie, other, ramp)
    size = meta_ref[SIZE_LANE : SIZE_LANE + 1, :]
    right = jnp.where(entry < size, right, 0.0)[:ROWS]
    side = rounded(jnp.where(zone_match()[None], right[:, None, :], 0.0).reshape(ROWS * Z, T * Z))
    step = jnp.where(tie, 0.5 * (current - other), 0.0)
    step = jnp.concatenate([step, jnp.zeros((W - RP, T * Z), jnp.float32)], axis=0).T
    out_ref[:, VP:] = rounded(step)
    total = lax.dot_general(side, hinv_ref[...], (((0,), (0,)), ((), ())), preferred_element_type=jnp.float32)
    out_ref[:, :V] = rounded(total)
    out_ref[:, V:VP] = jnp.zeros((T * Z, VP - V), jnp.bfloat16)


def last_sum_kernel(meta_ref, block_ref, dual_ref, primal_ref, dual_out_ref):
    total = jnp.zeros((Z, V), jnp.float32)
    for k in range(T):
        total = total + block_ref[k * Z : (k + 1) * Z, :V].astype(jnp.float32)
    primal_ref[:, 0, :] = total * live_rows(meta_ref)
    steps = []
    for k in range(-(-TIE // ROWS)):
        slot = ORDER.index(k)
        part = block_ref[slot * Z : (slot + 1) * Z, VP:].astype(jnp.float32)
        steps.append(part[:, : min(ROWS, TIE - k * ROWS)])
    dual_out_ref[:, 0, :] = dual_ref[...] + jnp.concatenate(steps, axis=1)


HBM = pl.BlockSpec(memory_space=pltpu.HBM)
VMEM = pl.BlockSpec(memory_space=pltpu.VMEM)


def call(kernel, name, in_specs, out_shape, scratch=(), out_spec=VMEM):
    many = isinstance(out_shape, tuple)
    return pl.pallas_call(
        kernel,
        name=name,
        in_specs=in_specs,
        out_specs=tuple(out_spec for _ in out_shape) if many else out_spec,
        out_shape=out_shape,
        scratch_shapes=scratch,
        compiler_params=pltpu.CompilerParams(vmem_limit_bytes=16 << 20),
    )


def near(values):
    return pltpu.with_memory_space_constraint(values, pltpu.VMEM)


def far(values):
    return pltpu.with_memory_space_constraint(values, pltpu.HBM)


def shards(x, duals, cost, hinv, sizes, partners):
    f32, bf16 = jnp.float32, jnp.bfloat16
    hinv = jnp.transpose(hinv, (1, 0, 2)).reshape(ROWS * Z, V)
    ties, last = call(
        tie_blocks_kernel,
        "tie_blocks",
        [HBM],
        (pltpu.HBM((MEMBERS * Z, W), f32), pltpu.HBM((Z, W), f32)),
        [pltpu.VMEM((ROUNDS, Z, W), f32)] + [pltpu.SemaphoreType.DMA((ROUNDS,))] * 2,
        HBM,
    )(far(x))
    ties = near(lax.all_to_all(ties, NEAR, 0, 0, tiled=True))
    last = near(lax.ppermute(last, "xl", [(0, 1), (1, 0)]))
    x, duals, cost, meta, hinv = call(
        fetch_kernel,
        "fetch",
        [HBM] * 6,
        (
            pltpu.VMEM((Z, 1, V), f32),
            pltpu.VMEM((Z, 1, TIE), f32),
            pltpu.VMEM((Z, 1, V), f32),
            pltpu.VMEM((META, W), jnp.int32),
            pltpu.VMEM((ROWS * Z, V), bf16),
        ),
        [pltpu.SMEM((Z,), jnp.int32), pltpu.SMEM((ROUNDS, Z), jnp.int32), pltpu.SemaphoreType.DMA((6,))],
    )(far(x), far(duals), far(cost), far(sizes), far(partners), far(hinv))
    block, dual = call(
        first_side_kernel,
        "first_side",
        [VMEM] * 6,
        (pltpu.VMEM((T * Z, BW), bf16), pltpu.VMEM((Z, TIE), f32)),
    )(meta, x, duals, cost, ties, last)
    block = near(lax.all_to_all(block, SLOTS, 0, 0, tiled=True))
    current, part = call(
        first_product_kernel,
        "first_product",
        [VMEM] * 3,
        (pltpu.VMEM((RP, T * Z), f32), pltpu.VMEM((SECOND_ROWS, T * Z), f32)),
    )(meta, block, hinv)
    two = near(lax.ppermute(part, AXES, swap_route(SECOND)))
    one = near(lax.ppermute(current, AXES, swap_route(FIRST)))
    block = call(second_product_kernel, "second_product", [VMEM] * 6, pltpu.VMEM((T * Z, DW), bf16))(
        meta, block, current, two, one, hinv
    )
    block = near(lax.all_to_all(block, SLOTS, 0, 0, tiled=True))
    shape = jax.ShapeDtypeStruct
    return call(last_sum_kernel, "last_sum", [VMEM] * 3, (shape((Z, 1, V), f32), shape((Z, 1, TIE), f32)))(
        meta, block, dual
    )


def solution(mesh):
    fine = Mesh(mesh.devices.reshape(SIZES), AXES)
    whole = P(ZONE, PERIOD, None)
    return jax.shard_map(
        shards,
        mesh=fine,
        in_specs=(whole, whole, whole, whole, P(ZONE), P(None, ZONE)),
        out_specs=(whole, whole),
        check_vma=False,
    )
```
